512 devices in a mesh: row: 16 (over y, core), col: 32 (over z, x).
Axes of the slice: x: 4, y: 8, z: 8, core: 2. Of those that a mesh axis runs over, the one named last changes fastest.
Arguments:
- matrix: float32 [4, 16, 256, 2, 32, 256], P(None, 'row', None, None, 'col'), as said below
- vectors: float32 [4, 16, 256, 256], P(None, 'row'), may hold values from -0.046875 to 0.046875
- t_factor: float32 [256, 256], replicated, as said below
Outputs:
- updated: float32 [4, 16, 256, 2, 32, 256], P(None, 'row', None, None, 'col')
The draws below stay inside these ranges and needn't reach their ends.
Inputs may be any that keep to these rules, and one draw needn't show every extreme that they name: matrix is exactly symmetric as an 16384 x 16384 matrix: entry (i, j) equals entry (j, i). t_factor is upper triangular with its diagonal between 0.5 and 1.5.
All inputs are finite; a program needn't handle non-finite values.
Results may differ from the reference program's by a relative error of at most 0.000068.
Values sent between devices are 32-bit elements; how exact they have to be, the bound alone decides.
A program may use at most 64 MiB of HBM per device.

```python
import jax
import jax.numpy as jnp
from jax import lax

NB = 256
LC = 2
LR = 4
N = 16384
N_ROW = 16
N_COL = 32


def draw_matrix(key, part):
    gauss = jax.random.normal(key, (N, N), jnp.float32)
    symmetric = (gauss + gauss.T) * 0.70710678
    return symmetric.reshape(LR, N_ROW, NB, LC, N_COL, NB)


def draw_t_factor(key, part):
    upper_part = jax.random.normal(key, (NB, NB), jnp.float32)
    upper_part = upper_part * NB ** (-0.5)
    diagonal_vals = jax.random.uniform(jax.random.fold_in(key, 3), (NB,), jnp.float32, 0.5, 1.5)
    return jnp.triu(upper_part, 1) + jnp.diag(diagonal_vals)


def block_levels(own_key, shape, shards, low, high):
    def one(axis_at, blocks):
        steps = jax.random.uniform(jax.random.fold_in(jax.random.fold_in(own_key, 6), axis_at), (blocks,), jnp.float32, low / len(shards), high / len(shards))
        return jnp.repeat(jnp.exp(steps), shape[axis_at] // blocks).reshape((-1,) + (1,) * (len(shape) - axis_at - 1))

    loudness = one(*shards[0])
    for cut in shards[1:]:
        loudness = loudness * one(*cut)
    return loudness


def noise(rng, extent, scale, reach, pieces=(), held_as=jnp.bfloat16):
    factor_of = block_levels(rng, extent, pieces, -0.22, 0.18) if pieces else 1.0
    values = jax.random.normal(rng, extent, jnp.float32) * scale * factor_of
    return jnp.minimum(jnp.maximum(values, -reach), reach).astype(held_as)


def setup_inputs(seed: int = 0) -> dict:
    splits = jax.random.split(jax.random.key(seed), 4)
    return {
        "matrix": draw_matrix(jax.random.fold_in(splits[3], 71), 0),
        "vectors": noise(splits[1], (LR, N_ROW, NB, NB), N ** -0.5, 0.046875, ((1, 16),), jnp.float32),
        "t_factor": draw_t_factor(jax.random.fold_in(splits[3], 71), 0),
    }


def product(left, right):
    return jnp.dot(left, right, precision=lax.Precision.HIGHEST, preferred_element_type=jnp.float32)


def reference(matrix, vectors, t_factor):
    matrix_full = matrix.reshape(N, N)
    vec_all = vectors.reshape(N, NB)
    top_block = jnp.tril(vec_all[:NB], -1) + jnp.eye(NB, dtype=vec_all.dtype)
    vec_all = jnp.concatenate([top_block, vec_all[NB:]], axis=0)
    applied = product(product(matrix_full, vec_all), t_factor)
    inner = product(vec_all.T, applied)
    middle = product(t_factor.T, inner)
    coupled = applied - 0.5 * product(vec_all, middle)
    result = matrix_full - product(vec_all, coupled.T) - product(coupled, vec_all.T)
    return result.reshape(matrix.shape)
```

```python
import jax
import jax.numpy as jnp
from jax import lax
from jax.experimental import pallas as pl
from jax.experimental.pallas import tpu as pltpu
from jax.sharding import PartitionSpec as P

F32 = jnp.float32
BF16 = jnp.bfloat16
MESH = pl.DeviceIdType.MESH
NN = (((1,), (0,)), ((), ()))
NT = (((1,), (1,)), ((), ()))
Y, Z, X = 8, 8, 4


def split(value):
    high = value.astype(BF16)
    return high, (value - high.astype(F32)).astype(BF16)


def dot3(left, right, dims):
    def dot(a, b):
        return lax.dot_general(a, b, dims, preferred_element_type=F32)

    return dot(left[0], right[0]) + (dot(left[0], right[1]) + dot(left[1], right[0]))


def unit_lower(block):
    i = lax.broadcasted_iota(jnp.int32, block.shape, 0)
    k = lax.broadcasted_iota(jnp.int32, block.shape, 1)
    return jnp.where(i > k, block, jnp.where(i == k, 1.0, 0.0).astype(F32))


def kernel(
    a_hbm, v_hbm, t_hbm, o_hbm,
    a_s, v_s, t_s, o_s, vth, vtl, uh, ul, qt, xbuf, rsrc, rs, pct, prt, vc,
    uch, ucl, gsrc, gz, gsum, gx, gt,
    ld_sem, out_sem, one_s, one_r, y_s, y_r, z_s, z_r, x_s, x_r, gx_s, gx_r,
):
    row = lax.axis_index("row")
    col = lax.axis_index("col")
    y, j = row // 2, row % 2
    z, x = col // X, col % X
    half, pos = col // 16, col % 16
    mine = 8 * j + y
    held = pos + 1 - 2 * (pos % 2)
    t_target = (pos, 16 * half + mine + 1 - 2 * (mine % 2))
    v_target = (2 * (held % 8) + held // 8, 16 * half + row)
    partner = (2 * y + 1 - j, col)

    def y_peer(d):
        return (2 * ((y + d) % Y) + j, col)

    def z_peer(d):
        return (row, X * ((z + d) % Z) + x)

    def x_peer(d):
        return (row, X * z + (x + d) % X)

    def rows(start, size, step=16):
        return pl.ds(pl.multiple_of(start, step), size)

    started = []

    def send(src, dst, ssem, rsem, target):
        copy = pltpu.make_async_remote_copy(
            src_ref=src, dst_ref=dst, send_sem=ssem, recv_sem=rsem,
            device_id={"row": target[0], "col": target[1]}, device_id_type=MESH,
        )
        copy.start()
        started.append(copy)
        return copy

    load_v = pltpu.make_async_copy(v_hbm, v_s, ld_sem.at[4])
    load_v.start()
    load_t = pltpu.make_async_copy(t_hbm, t_s, ld_sem.at[5])

    def load_a(lr):
        part = rows(lr * 1024, 1024, 1024)
        return pltpu.make_async_copy(a_hbm.at[part], a_s.at[part], ld_sem.at[lr])

    for lr in range(4):
        load_a(lr).start()
    load_t.start()

    barrier = pltpu.get_barrier_semaphore()
    greeted = (
        [y_peer(d) for d in range(1, Y)] + [z_peer(d) for d in range(1, Z)]
        + [x_peer(d) for d in range(1, X)] + [partner, t_target, v_target]
    )
    for peer in greeted:
        pl.semaphore_signal(
            barrier, inc=1, device_id={"row": peer[0], "col": peer[1]}, device_id_type=MESH
        )

    load_v.wait()

    @pl.loop(0, 4)
    def _(lr):
        block = v_s[lr]
        fixed = jnp.where(row * 4 + lr == 0, unit_lower(block), block)
        high, low = split(fixed.T)
        vth[lr] = high
        vtl[lr] = low
        high, low = split(fixed)
        uh[lr] = high
        ul[lr] = low

    qt[...] = jnp.zeros_like(qt)

    @pl.loop(0, 4)
    def _(lr):
        load_a(lr).wait()
        left = (vth[lr], vtl[lr])
        for lc in range(2):
            block = jnp.concatenate(
                [a_s[pl.ds(lr * 1024 + 2 * lc + q, 256, stride=4), :] for q in range(2)], axis=1
            )
            qt[:, 256 * lc : 256 * lc + 256] += dot3(left, split(block), NN)

    pl.semaphore_wait(barrier, len(greeted))

    swap = send(qt.at[rows(128 * (1 - j), 128)], xbuf, one_s.at[0], one_r.at[0], partner)
    v_move = send(
        v_s.at[half + 2 * (held // 8), rows(32 * (held % 8), 32)],
        vc.at[rows(32 * held, 32)], one_s.at[1], one_r.at[1], v_target,
    )
    load_t.wait()
    swap.wait_recv()
    rsrc[...] = qt[rows(128 * j, 128), :] + xbuf[...]
    order = (4, 3, 5, 2, 6, 1, 7)
    scatter = [
        send(
            rsrc.at[rows(16 * ((y + d) % Y), 16)], rs.at[d],
            y_s.at[0, d], y_r.at[0, d], y_peer(d),
        )
        for d in order
    ]
    factor = split(t_s[...])

    @pl.loop(0, 4)
    def _(lr):
        high, low = split(dot3((uh[lr], ul[lr]), factor, NT))
        uh[lr] = high
        ul[lr] = low

    v_move.wait_recv()
    v_part = vc.at[rows(32 * mine, 32)]
    v_gather = [
        send(v_part, v_part, y_s.at[1, d], y_r.at[1, d], y_peer(d)) for d in order
    ]
    total = rsrc[rows(16 * y, 16), :]
    for copy, d in zip(scatter, order):
        copy.wait_recv()
        total = total + rs[d]
    own = rows(16 * mine, 16)
    pct[own, :] = total
    t_move = send(
        pct.at[own], prt.at[half, own], one_s.at[2], one_r.at[2], t_target
    )
    p_gather = [
        send(pct.at[own], pct.at[own], y_s.at[2, d], y_r.at[2, d], y_peer(d)) for d in order
    ]
    for copy in v_gather:
        copy.wait_recv()
    v_half = vc.at[rows(256 * j, 256)]
    v_swap = send(v_half, v_half, one_s.at[3], one_r.at[3], partner)

    t_move.wait_recv()
    chunk = prt.at[half, rows(16 * held, 16)]
    z_gather = {
        d: send(chunk, chunk, z_s.at[0, d], z_r.at[0, d], z_peer(d)) for d in order
    }

    def chunk_of(zi, xi):
        p = 4 * (zi % 4) + xi
        return prt.at[zi // 4, rows(16 * (p + 1 - 2 * (p % 2)), 16)]

    def half_of(zi, xi, which):
        p = 4 * (zi % 4) + xi
        return prt.at[zi // 4, rows(16 * (p + 1 - 2 * (p % 2)) + 8 * which, 8, 8)]

    def x_send(d):
        part = chunk_of((z - d) % Z, x)
        return [
            send(part, part, x_s.at[side, d], x_r.at[side, d], x_peer(1 - 2 * side))
            for side in range(2)
        ]

    x_gather = {0: x_send(0)}

    v_swap.wait_recv()

    first = vc[0:256, :]
    first = jnp.where(col == 0, unit_lower(first), first)
    v_cols = split(jnp.concatenate([first, vc[256:512, :]], axis=0))
    gsrc[...] = dot3(split(total), v_cols, NN)
    g_z = [send(gsrc, gz.at[d], z_s.at[1, d], z_r.at[1, d], z_peer(d)) for d in order]

    for d in (1, 7, 2, 6, 3, 5, 4):
        z_gather[d].wait_recv()
        x_gather[d] = x_send(d)

    high, low = split(dot3(factor, v_cols, NT))
    uch[...] = high
    ucl[...] = low

    for copy in p_gather:
        copy.wait_recv()
    p_half = pct.at[rows(128 * j, 128)]
    p_swap = send(p_half, p_half, one_s.at[4], one_r.at[4], partner)

    part_sum = gsrc[...]
    for copy, d in zip(g_z, order):
        copy.wait_recv()
        part_sum = part_sum + gz[d]
    gsum[...] = part_sum
    g_x = [
        send(gsum, gx.at[d], gx_s.at[d], gx_r.at[d], x_peer(d)) for d in range(1, X)
    ]

    forward = []
    for d in (0, 1, 7, 2, 6, 3, 5, 4):
        for side in range(2):
            x_gather[d][side].wait_recv()
            part = half_of((z - d) % Z, (x - 1 + 2 * side) % X, side)
            forward.append(
                send(part, part, x_s.at[2 + side, d], x_r.at[2 + side, d], x_peer(1 - 2 * side))
            )

    part_sum = gsum[...]
    for d, copy in zip(range(1, X), g_x):
        copy.wait_recv()
        part_sum = part_sum + gx[d]
    gt[own, :] = part_sum
    g_gather = [
        send(gt.at[own], gt.at[own], y_s.at[3, d], y_r.at[3, d], y_peer(d)) for d in order
    ]

    for copy in forward:
        copy.wait_recv()

    @pl.loop(0, 4)
    def _(lr):
        h = lr % 2
        left = split(prt[h, :, pl.ds(pl.multiple_of(256 * (lr // 2), 256), 256)].T)
        for lc in range(2):
            cols = slice(256 * lc, 256 * lc + 256)
            delta = dot3(left, (uch[:, cols], ucl[:, cols]), NN)
            for q in range(2):
                where = pl.ds(lr * 1024 + 2 * lc + q, 256, stride=4)
                o_s[where, :] = a_s[where, :] - delta[:, 128 * q : 128 * q + 128]

    for copy in g_gather:
        copy.wait_recv()
    g_half = gt.at[rows(128 * j, 128)]
    g_swap = send(g_half, g_half, one_s.at[5], one_r.at[5], partner)
    p_swap.wait_recv()
    g_swap.wait_recv()
    coupled = split(pct[...] - dot3(split(gt[...]), (uch[...], ucl[...]), NN))
    uch[...] = coupled[0]
    ucl[...] = coupled[1]

    def store(lr):
        part = rows(lr * 1024, 1024, 1024)
        return pltpu.make_async_copy(o_s.at[part], o_hbm.at[part], out_sem.at[lr])

    @pl.loop(0, 4)
    def _(lr):
        left = (uh[lr], ul[lr])
        for lc in range(2):
            cols = slice(256 * lc, 256 * lc + 256)
            delta = dot3(left, (uch[:, cols], ucl[:, cols]), NN)
            for q in range(2):
                where = pl.ds(lr * 1024 + 2 * lc + q, 256, stride=4)
                o_s[where, :] = o_s[where, :] - delta[:, 128 * q : 128 * q + 128]
        store(lr).start()

    for copy in started:
        copy.wait_send()
    for lr in range(4):
        store(lr).wait()


def per_device(matrix, vectors, t_factor):
    a = matrix.reshape(4096, 128)
    v = vectors.reshape(4, 256, 256)
    vm = pltpu.VMEM
    dma = pltpu.SemaphoreType.DMA
    out = pl.pallas_call(
        kernel,
        out_shape=jax.ShapeDtypeStruct((4096, 128), F32),
        in_specs=[pl.BlockSpec(memory_space=pl.ANY)] * 3,
        out_specs=pl.BlockSpec(memory_space=pl.ANY),
        scratch_shapes=[
            vm((4096, 128), F32), vm((4, 256, 256), F32), vm((256, 256), F32),
            vm((4096, 128), F32),
            vm((4, 256, 256), BF16), vm((4, 256, 256), BF16),
            vm((4, 256, 256), BF16), vm((4, 256, 256), BF16),
            vm((256, 512), F32), vm((128, 512), F32), vm((128, 512), F32),
            vm((8, 16, 512), F32), vm((256, 512), F32), vm((2, 256, 512), F32),
            vm((512, 256), F32), vm((256, 512), BF16), vm((256, 512), BF16),
            vm((16, 256), F32), vm((8, 16, 256), F32), vm((16, 256), F32),
            vm((4, 16, 256), F32), vm((256, 256), F32),
            dma((6,)), dma((4,)), dma((6,)), dma((6,)), dma((4, 8)), dma((4, 8)),
            dma((2, 8)), dma((2, 8)), dma((4, 8)), dma((4, 8)), dma((4,)), dma((4,)),
        ],
        compiler_params=pltpu.CompilerParams(collective_id=0, has_side_effects=True),
        name="band_update",
    )(a, v, t_factor)
    return out.reshape(matrix.shape)


def solution(mesh):
    in_specs = (P(None, "row", None, None, "col", None), P(None, "row", None, None), P())
    out_specs = P(None, "row", None, None, "col", None)
    return jax.shard_map(
        per_device, mesh=mesh, in_specs=in_specs, out_specs=out_specs, check_vma=False
    )
```

```python
import jax
import jax.numpy as jnp
from jax import lax
from jax.experimental import pallas as pl
from jax.experimental.pallas import tpu as pltpu
from jax.sharding import PartitionSpec as P

F32 = jnp.float32
BF16 = jnp.bfloat16
MESH = pl.DeviceIdType.MESH
NN = (((1,), (0,)), ((), ()))
NT = (((1,), (1,)), ((), ()))
Y, Z, X = 8, 8, 4
VMEM_LIMIT = 24 * 1024 * 1024


def split(value):
    high = value.astype(BF16)
    return high, (value - high.astype(F32)).astype(BF16)


def dot3(left, right, dims):
    def dot(a, b):
        return lax.dot_general(a, b, dims, preferred_element_type=F32)

    return dot(left[0], right[0]) + (dot(left[0], right[1]) + dot(left[1], right[0]))


def unit_lower(block):
    i = lax.broadcasted_iota(jnp.int32, block.shape, 0)
    k = lax.broadcasted_iota(jnp.int32, block.shape, 1)
    return jnp.where(i > k, block, jnp.where(i == k, 1.0, 0.0).astype(F32))


def kernel(
    a_s, v_s, t_s, o_s, uh, ul, wh, wl,
    vth, vtl, qt, xbuf, rsrc, rs, pct, prt, vc, uch, ucl, gsrc, gz, gsum, gx, gt,
    one_s, one_r, v_s_s, v_s_r, rs_s, rs_r, y_s, y_r,
    z_s, z_r, gz_s, gz_r, x_s, x_r, f_s, f_r, gx_s, gx_r,
):
    row = lax.axis_index("row")
    col = lax.axis_index("col")
    y, j = row // 2, row % 2
    z, x = col // X, col % X
    half, pos = col // 16, col % 16

    def flip(index):
        return index + 1 - 2 * (index % 2)

    def slice_at(position):
        other = flip(position)
        return 8 * (other % 2) + other // 2

    mine, held = 8 * j + y, slice_at(pos)
    t_target, t_source = (pos, 16 * half + flip(row)), (flip(pos), 16 * half + row)
    partner = (2 * y + 1 - j, col)

    def y_peer(d):
        return (2 * ((y + d) % Y) + j, col)

    def z_peer(d):
        return (row, X * ((z + d) % Z) + x)

    def x_peer(d):
        return (row, X * z + (x + d) % X)

    def v_target(d):
        return (2 * ((held + d) % Y) + held // 8, 16 * half + row)

    def rows(start, size, step=16):
        return pl.ds(pl.multiple_of(start, step), size)

    started = []

    def send(src, dst, ssem, rsem, target):
        copy = pltpu.make_async_remote_copy(
            src_ref=src, dst_ref=dst, send_sem=ssem, recv_sem=rsem,
            device_id={"row": target[0], "col": target[1]}, device_id_type=MESH,
        )
        copy.start()
        started.append(copy)
        return copy

    barrier = pltpu.get_barrier_semaphore()
    greeted = (
        [y_peer(d) for d in range(1, Y)] + [z_peer(d) for d in range(1, Z)]
        + [x_peer(d) for d in range(1, X)] + [partner, t_source]
        + [(pos, 16 * half + 2 * i + 1 - j) for i in range(8)]
    )
    for peer in greeted:
        pl.semaphore_signal(
            barrier, inc=1, device_id={"row": peer[0], "col": peer[1]}, device_id_type=MESH
        )

    for lr in range(4):
        block = v_s[lr]
        if lr == 0:
            block = jnp.where(row == 0, unit_lower(block), block)
        high, low = split(block.T)
        vth[:, 256 * lr : 256 * lr + 256] = high
        vtl[:, 256 * lr : 256 * lr + 256] = low
        high, low = split(block)
        uh[lr] = high
        ul[lr] = low

    def partial(lc):
        block = jnp.concatenate(
            [a_s[pl.ds(2 * lc + q, 1024, stride=4), :] for q in range(2)], axis=1
        )
        qt[lc] = dot3((vth[...], vtl[...]), split(block), NN)

    def swap_of(lc):
        return send(
            qt.at[lc, rows(128 * (1 - j), 128)], xbuf.at[lc],
            one_s.at[lc], one_r.at[lc], partner,
        )

    order = (4, 3, 5, 2, 6, 1, 7)

    partial(0)
    pl.semaphore_wait(barrier, len(greeted))
    swaps = [swap_of(0)]
    v_part = v_s.at[half + 2 * (held // 8), rows(32 * (held % 8), 32)]
    v_moves = [
        send(v_part, vc.at[rows(32 * held, 32)], v_s_s.at[d], v_s_r.at[d], v_target(d))
        for d in range(8)
    ]
    partial(1)
    swaps.append(swap_of(1))
    scatter = []
    for lc in range(2):
        swaps[lc].wait_recv()
        rsrc[lc] = qt[lc, rows(128 * j, 128), :] + xbuf[lc]
        scatter.append([
            send(
                rsrc.at[lc, rows(16 * ((y + d) % Y), 16)], rs.at[lc, d],
                rs_s.at[lc, d], rs_r.at[lc, d], y_peer(d),
            )
            for d in order
        ])
    factor = split(t_s[...])
    for lr in range(4):
        high, low = split(dot3((uh[lr], ul[lr]), factor, NT))
        uh[lr] = high
        ul[lr] = low
    own = rows(16 * mine, 16)
    totals, t_moves = [], []
    for lc in range(2):
        total = rsrc[lc, rows(16 * y, 16), :]
        for copy, d in zip(scatter[lc], order):
            copy.wait_recv()
            total = total + rs[lc, d]
        pct[lc, own, :] = total
        totals.append(total)
        t_moves.append(send(
            pct.at[lc, own], prt.at[half, lc, own], one_s.at[2 + lc], one_r.at[2 + lc], t_target
        ))
    p_part = pct.at[:, own]
    p_gather = [
        send(p_part, p_part, y_s.at[0, d], y_r.at[0, d], y_peer(d)) for d in order
    ]
    for copy in v_moves:
        copy.wait_recv()
    v_half = vc.at[rows(256 * j, 256)]
    v_swap = send(v_half, v_half, one_s.at[4], one_r.at[4], partner)
    v_swap.wait_recv()
    first = vc[0:256, :]
    first = jnp.where(col == 0, unit_lower(first), first)
    v_cols = [split(first), split(vc[256:512, :])]
    gsrc[...] = dot3(split(totals[0]), v_cols[0], NN) + dot3(split(totals[1]), v_cols[1], NN)
    g_z = [send(gsrc, gz.at[d], gz_s.at[d], gz_r.at[d], z_peer(d)) for d in order]
    for lc in range(2):
        high, low = split(dot3(factor, v_cols[lc], NT))
        uch[:, 256 * lc : 256 * lc + 256] = high
        ucl[:, 256 * lc : 256 * lc + 256] = low

    def chunk_of(zi, xi, lc):
        return prt.at[zi // 4, lc, rows(16 * slice_at(4 * (zi % 4) + xi), 16)]

    def x_send(d, lc):
        part = chunk_of((z - d) % Z, x, lc)
        return [
            send(part, part, x_s.at[side, lc, d], x_r.at[side, lc, d], x_peer(1 - 2 * side))
            for side in range(2)
        ]

    z_gather, x_gather = [], [{}, {}]
    for lc in range(2):
        t_moves[lc].wait_recv()
        chunk = chunk_of(z, x, lc)
        z_gather.append({
            d: send(chunk, chunk, z_s.at[lc, d], z_r.at[lc, d], z_peer(d)) for d in order
        })
        x_gather[lc][0] = x_send(0, lc)
    near = (1, 7, 2, 6, 3, 5, 4)
    forward = [[], []]

    def pass_on(d, lc):
        x_gather[lc][d][lc].wait_recv()
        part = chunk_of((z - d) % Z, (x - 1 + 2 * lc) % X, lc)
        forward[lc].append(
            send(part, part, f_s.at[lc, d], f_r.at[lc, d], x_peer(1 - 2 * lc))
        )

    for d in near:
        z_gather[0][d].wait_recv()
        x_gather[0][d] = x_send(d, 0)
    for d in near:
        z_gather[1][d].wait_recv()
        x_gather[1][d] = x_send(d, 1)
    part_sum = gsrc[...]
    for copy, d in zip(g_z, order):
        copy.wait_recv()
        part_sum = part_sum + gz[d]
    gsum[...] = part_sum
    g_x = [
        send(gsum, gx.at[d], gx_s.at[d], gx_r.at[d], x_peer(d)) for d in range(1, X)
    ]
    for d in (0,) + near:
        pass_on(d, 0)
    for d in (0,) + near:
        pass_on(d, 1)
    for d, copy in zip(range(1, X), g_x):
        copy.wait_recv()
        part_sum = part_sum + gx[d]
    gt[own, :] = part_sum
    g_gather = [
        send(gt.at[own], gt.at[own], y_s.at[1, d], y_r.at[1, d], y_peer(d)) for d in order
    ]
    for copy in p_gather:
        copy.wait_recv()
    p_half = pct.at[:, rows(128 * j, 128)]
    p_swap = send(p_half, p_half, one_s.at[5], one_r.at[5], partner)

    for lc in range(2):
        for d in (0,) + near:
            x_gather[lc][d][1 - lc].wait_recv()
        for copy in forward[lc]:
            copy.wait_recv()
        for h in range(2):
            lr = h + 2 * lc
            left = split(prt[h, lc].T)
            for oc in range(2):
                cols = slice(256 * oc, 256 * oc + 256)
                delta = dot3(left, (uch[:, cols], ucl[:, cols]), NN)
                for q in range(2):
                    where = pl.ds(lr * 1024 + 2 * oc + q, 256, stride=4)
                    o_s[where, :] = a_s[where, :] - delta[:, 128 * q : 128 * q + 128]
    for copy in g_gather:
        copy.wait_recv()
    g_half = gt.at[rows(128 * j, 128)]
    g_swap = send(g_half, g_half, one_s.at[6], one_r.at[6], partner)
    p_swap.wait_recv()
    g_swap.wait_recv()
    inner = split(gt[...])
    for lc in range(2):
        cols = slice(256 * lc, 256 * lc + 256)
        high, low = split(pct[lc] - dot3(inner, (uch[:, cols], ucl[:, cols]), NN))
        wh[:, cols] = high
        wl[:, cols] = low
    for copy in started:
        copy.wait_send()


def finish_kernel(o_ref, uh_ref, ul_ref, wh_ref, wl_ref, out_ref):
    left = (uh_ref[0], ul_ref[0])
    count = left[0].shape[0]
    for oc in range(2):
        cols = slice(256 * oc, 256 * oc + 256)
        delta = dot3(left, (wh_ref[:, cols], wl_ref[:, cols]), NN)
        for q in range(2):
            where = pl.ds(2 * oc + q, count, stride=4)
            out_ref[where, :] = o_ref[where, :] - delta[:, 128 * q : 128 * q + 128]


def per_device(matrix, vectors, t_factor):
    a = matrix.reshape(4096, 128)
    v = vectors.reshape(4, 256, 256)
    vm = pltpu.VMEM
    dma = pltpu.SemaphoreType.DMA
    shape = jax.ShapeDtypeStruct
    parts = pl.pallas_call(
        kernel,
        out_shape=[
            shape((4096, 128), F32), shape((4, 256, 256), BF16), shape((4, 256, 256), BF16),
            shape((256, 512), BF16), shape((256, 512), BF16),
        ],
        in_specs=[pl.BlockSpec(memory_space=pltpu.VMEM)] * 3,
        out_specs=[pl.BlockSpec(memory_space=pltpu.VMEM)] * 5,
        scratch_shapes=[
            vm((256, 1024), BF16), vm((256, 1024), BF16),
            vm((2, 256, 256), F32), vm((2, 128, 256), F32), vm((2, 128, 256), F32),
            vm((2, 8, 16, 256), F32), vm((2, 256, 256), F32), vm((2, 2, 256, 256), F32),
            vm((512, 256), F32), vm((256, 512), BF16), vm((256, 512), BF16),
            vm((16, 256), F32), vm((8, 16, 256), F32), vm((16, 256), F32),
            vm((4, 16, 256), F32), vm((256, 256), F32),
            dma((7,)), dma((7,)), dma((8,)), dma((8,)),
            dma((2, 8)), dma((2, 8)), dma((2, 8)), dma((2, 8)),
            dma((2, 8)), dma((2, 8)), dma((8,)), dma((8,)),
            dma((2, 2, 8)), dma((2, 2, 8)), dma((2, 8)), dma((2, 8)), dma((4,)), dma((4,)),
        ],
        compiler_params=pltpu.CompilerParams(
            collective_id=0, has_side_effects=True, vmem_limit_bytes=VMEM_LIMIT
        ),
        name="band_update",
    )(a, v, t_factor)
    steps = 8
    out = pl.pallas_call(
        finish_kernel,
        grid=(steps,),
        out_shape=shape((4096, 128), F32),
        in_specs=[
            pl.BlockSpec((4096 // steps, 128), lambda i: (i, 0)),
            pl.BlockSpec((1, 1024 // steps, 256), lambda i: (i // 2, i % 2, 0)),
            pl.BlockSpec((1, 1024 // steps, 256), lambda i: (i // 2, i % 2, 0)),
            pl.BlockSpec((256, 512), lambda i: (0, 0)),
            pl.BlockSpec((256, 512), lambda i: (0, 0)),
        ],
        out_specs=pl.BlockSpec((4096 // steps, 128), lambda i: (i, 0)),
        compiler_params=pltpu.CompilerParams(vmem_limit_bytes=VMEM_LIMIT // 2),
        name="band_finish",
    )(*parts)
    return out.reshape(matrix.shape)


def solution(mesh):
    in_specs = (P(None, "row", None, None, "col", None), P(None, "row", None, None), P())
    out_specs = P(None, "row", None, None, "col", None)
    return jax.shard_map(
        per_device, mesh=mesh, in_specs=in_specs, out_specs=out_specs, check_vma=False
    )
```

```python
import jax
import jax.numpy as jnp
from jax import lax
from jax.experimental import pallas as pl
from jax.experimental.pallas import tpu as pltpu
from jax.sharding import PartitionSpec as P

F32 = jnp.float32
BF16 = jnp.bfloat16
MESH = pl.DeviceIdType.MESH
NN = (((1,), (0,)), ((), ()))
NT = (((1,), (1,)), ((), ()))
Y, Z, X = 8, 8, 4
VMEM_LIMIT = 24 * 1024 * 1024


def rem(value, by):
    return lax.rem(value, jnp.int32(by))


def div(value, by):
    return lax.div(value, jnp.int32(by))


def split(value):
    high = value.astype(BF16)
    return high, (value - high.astype(F32)).astype(BF16)


def dot3(left, right, dims):
    def dot(a, b):
        return lax.dot_general(a, b, dims, preferred_element_type=F32)

    return dot(left[0], right[0]) + (dot(left[0], right[1]) + dot(left[1], right[0]))


def unit_lower(block):
    i = lax.broadcasted_iota(jnp.int32, block.shape, 0)
    k = lax.broadcasted_iota(jnp.int32, block.shape, 1)
    return jnp.where(i > k, block, jnp.where(i == k, 1.0, 0.0).astype(F32))


def kernel(
    a_hbm, v_hbm, t_hbm, o_s, uh, ul, wh, wl, a_s, v_s, t_s,
    vth, vtl, qt, xbuf, rsrc, rs, pct, prt, vc, uch, ucl, gsrc, gz, gsum, gx, gt,
    ld_sem, one_s, one_r, v_s_s, v_s_r, rs_s, rs_r, y_s, y_r,
    z_s, z_r, gz_s, gz_r, x_s, x_r, f_s, f_r, gx_s, gx_r,
):
    row = lax.axis_index("row")
    col = lax.axis_index("col")
    y, j = div(row, 2), rem(row, 2)
    z, x = div(col, X), rem(col, X)
    half, pos = div(col, 16), rem(col, 16)
    zs = [rem(z + Z - d, Z) for d in range(Z)]
    xs = [rem(x + d, X) for d in range(X)]
    ys = [rem(y + d, Y) for d in range(Y)]

    def flip(index):
        return index + 1 - 2 * rem(index, 2)

    def slice_at(position):
        other = flip(position)
        return 8 * rem(other, 2) + div(other, 2)

    mine, held = 8 * j + y, slice_at(pos)
    t_target, t_source = (pos, 16 * half + flip(row)), (flip(pos), 16 * half + row)
    partner = (2 * y + 1 - j, col)

    def y_peer(d):
        return (2 * ys[d] + j, col)

    def z_peer(d):
        return (row, X * zs[Z - d] + x)

    def x_peer(d):
        return (row, X * z + xs[d % X])

    def v_target(d):
        return (2 * rem(held + d, Y) + div(held, 8), 16 * half + row)

    def rows(start, size, step=16):
        return pl.ds(pl.multiple_of(start, step), size)

    started = []

    def send(src, dst, ssem, rsem, target):
        copy = pltpu.make_async_remote_copy(
            src_ref=src, dst_ref=dst, send_sem=ssem, recv_sem=rsem,
            device_id={"row": target[0], "col": target[1]}, device_id_type=MESH,
        )
        copy.start()
        started.append(copy)
        return copy

    loads = [
        pltpu.make_async_copy(src, dst, ld_sem.at[i])
        for i, (src, dst) in enumerate([(v_hbm, v_s), (a_hbm, a_s), (t_hbm, t_s)])
    ]
    for copy in loads:
        copy.start()
    barrier = pltpu.get_barrier_semaphore()
    greeted = (
        [y_peer(d) for d in range(1, Y)] + [z_peer(d) for d in range(1, Z)]
        + [x_peer(d) for d in range(1, X)] + [partner, t_source]
        + [(pos, 16 * half + 2 * i + 1 - j) for i in range(8)]
    )
    for peer in greeted:
        pl.semaphore_signal(
            barrier, inc=1, device_id={"row": peer[0], "col": peer[1]}, device_id_type=MESH
        )

    loads[0].wait()
    for lr in range(4):
        block = v_s[lr]
        if lr == 0:
            block = jnp.where(row == 0, unit_lower(block), block)
        high, low = split(block.T)
        vth[:, 256 * lr : 256 * lr + 256] = high
        vtl[:, 256 * lr : 256 * lr + 256] = low
        high, low = split(block)
        uh[lr] = high
        ul[lr] = low

    loads[1].wait()

    def partial(lc):
        block = jnp.concatenate(
            [a_s[pl.ds(2 * lc + q, 1024, stride=4), :] for q in range(2)], axis=1
        )
        qt[lc] = dot3((vth[...], vtl[...]), split(block), NN)

    def swap_of(lc):
        return send(
            qt.at[lc, rows(128 * (1 - j), 128)], xbuf.at[lc],
            one_s.at[lc], one_r.at[lc], partner,
        )

    order = (4, 3, 5, 2, 6, 1, 7)

    partial(0)
    pl.semaphore_wait(barrier, len(greeted))
    swaps = [swap_of(0)]
    v_part = v_s.at[half + 2 * div(held, 8), rows(32 * rem(held, 8), 32)]
    v_moves = [
        send(v_part, vc.at[rows(32 * held, 32)], v_s_s.at[d], v_s_r.at[d], v_target(d))
        for d in range(8)
    ]
    partial(1)
    swaps.append(swap_of(1))
    scatter = []
    for lc in range(2):
        swaps[lc].wait_recv()
        rsrc[lc] = qt[lc, rows(128 * j, 128), :] + xbuf[lc]
        scatter.append([
            send(
                rsrc.at[lc, rows(16 * ys[d], 16)], rs.at[lc, d],
                rs_s.at[lc, d], rs_r.at[lc, d], y_peer(d),
            )
            for d in order
        ])
    loads[2].wait()
    factor = split(t_s[...])
    for lr in range(4):
        high, low = split(dot3((uh[lr], ul[lr]), factor, NT))
        uh[lr] = high
        ul[lr] = low
    own = rows(16 * mine, 16)
    t_z, t_x = 4 * half + div(flip(row), X), rem(flip(row), X)
    totals, t_moves = [], []
    for lc in range(2):
        total = rsrc[lc, rows(16 * y, 16), :]
        for copy, d in zip(scatter[lc], order):
            copy.wait_recv()
            total = total + rs[lc, d]
        pct[lc, own, :] = total
        totals.append(total)
        t_moves.append(send(
            pct.at[lc, own], prt.at[lc, t_z, t_x], one_s.at[2 + lc], one_r.at[2 + lc], t_target
        ))
    p_part = pct.at[:, own]
    p_gather = [
        send(p_part, p_part, y_s.at[0, d], y_r.at[0, d], y_peer(d)) for d in order
    ]
    for copy in v_moves:
        copy.wait_recv()
    v_half = vc.at[rows(256 * j, 256)]
    v_swap = send(v_half, v_half, one_s.at[4], one_r.at[4], partner)
    v_swap.wait_recv()
    first = vc[0:256, :]
    first = jnp.where(col == 0, unit_lower(first), first)
    v_cols = [split(first), split(vc[256:512, :])]
    gsrc[...] = dot3(split(totals[0]), v_cols[0], NN) + dot3(split(totals[1]), v_cols[1], NN)
    g_z = [send(gsrc, gz.at[d], gz_s.at[d], gz_r.at[d], z_peer(d)) for d in order]
    for lc in range(2):
        high, low = split(dot3(factor, v_cols[lc], NT))
        uch[:, 256 * lc : 256 * lc + 256] = high
        ucl[:, 256 * lc : 256 * lc + 256] = low

    def x_send(d, lc):
        part = prt.at[lc, zs[d], x]
        return [
            send(part, part, x_s.at[side, lc, d], x_r.at[side, lc, d], x_peer(1 - 2 * side))
            for side in range(2)
        ]

    z_gather, x_gather = [], [{}, {}]
    for lc in range(2):
        t_moves[lc].wait_recv()
        chunk = prt.at[lc, z, x]
        z_gather.append({
            d: send(chunk, chunk, z_s.at[lc, d], z_r.at[lc, d], z_peer(d)) for d in order
        })
        x_gather[lc][0] = x_send(0, lc)
    near = (1, 7, 2, 6, 3, 5, 4)
    forward = [[], []]

    def pass_on(d, lc):
        x_gather[lc][d][lc].wait_recv()
        part = prt.at[lc, zs[d], xs[3 - 2 * lc]]
        forward[lc].append(
            send(part, part, f_s.at[lc, d], f_r.at[lc, d], x_peer(1 - 2 * lc))
        )

    for d in near:
        z_gather[0][d].wait_recv()
        x_gather[0][d] = x_send(d, 0)
    for d in near:
        z_gather[1][d].wait_recv()
        x_gather[1][d] = x_send(d, 1)
    part_sum = gsrc[...]
    for copy, d in zip(g_z, order):
        copy.wait_recv()
        part_sum = part_sum + gz[d]
    gsum[...] = part_sum
    g_x = [
        send(gsum, gx.at[d], gx_s.at[d], gx_r.at[d], x_peer(d)) for d in range(1, X)
    ]
    for d in (0,) + near:
        pass_on(d, 0)
    for d in (0,) + near:
        pass_on(d, 1)
    for d, copy in zip(range(1, X), g_x):
        copy.wait_recv()
        part_sum = part_sum + gx[d]
    gt[own, :] = part_sum
    g_gather = [
        send(gt.at[own], gt.at[own], y_s.at[1, d], y_r.at[1, d], y_peer(d)) for d in order
    ]
    for copy in p_gather:
        copy.wait_recv()
    p_half = pct.at[:, rows(128 * j, 128)]
    p_swap = send(p_half, p_half, one_s.at[5], one_r.at[5], partner)

    places = [(2 * (e % 8) + e // 8) ^ 1 for e in range(16)]
    for lc in range(2):
        for d in (0,) + near:
            x_gather[lc][d][1 - lc].wait_recv()
        for copy in forward[lc]:
            copy.wait_recv()
        for h in range(2):
            lr = h + 2 * lc
            left = split(jnp.concatenate(
                [prt[lc, 4 * h + p // X, p % X] for p in places], axis=0
            ).T)
            for oc in range(2):
                cols = slice(256 * oc, 256 * oc + 256)
                delta = dot3(left, (uch[:, cols], ucl[:, cols]), NN)
                for q in range(2):
                    where = pl.ds(lr * 1024 + 2 * oc + q, 256, stride=4)
                    o_s[where, :] = a_s[where, :] - delta[:, 128 * q : 128 * q + 128]
    for copy in g_gather:
        copy.wait_recv()
    g_half = gt.at[rows(128 * j, 128)]
    g_swap = send(g_half, g_half, one_s.at[6], one_r.at[6], partner)
    p_swap.wait_recv()
    g_swap.wait_recv()
    inner = split(gt[...])
    for lc in range(2):
        cols = slice(256 * lc, 256 * lc + 256)
        high, low = split(pct[lc] - dot3(inner, (uch[:, cols], ucl[:, cols]), NN))
        wh[:, cols] = high
        wl[:, cols] = low
    for copy in started:
        copy.wait_send()


def finish_kernel(o_ref, uh_ref, ul_ref, wh_ref, wl_ref, out_hbm, buf, sems):
    def store(lr):
        part = pl.ds(1024 * lr, 1024)
        return pltpu.make_async_copy(buf.at[part], out_hbm.at[part], sems.at[lr])

    right = [
        (wh_ref[:, 256 * oc : 256 * oc + 256], wl_ref[:, 256 * oc : 256 * oc + 256])
        for oc in range(2)
    ]
    for lr in range(4):
        left = (uh_ref[lr], ul_ref[lr])
        for oc in range(2):
            delta = dot3(left, right[oc], NN)
            for q in range(2):
                where = pl.ds(1024 * lr + 2 * oc + q, 256, stride=4)
                buf[where, :] = o_ref[where, :] - delta[:, 128 * q : 128 * q + 128]
        store(lr).start()
    for lr in range(4):
        store(lr).wait()


def per_device(matrix, vectors, t_factor):
    a = matrix.reshape(4096, 128)
    v = vectors.reshape(4, 256, 256)
    vm = pltpu.VMEM
    dma = pltpu.SemaphoreType.DMA
    shape = jax.ShapeDtypeStruct
    parts = pl.pallas_call(
        kernel,
        out_shape=[
            shape((4096, 128), F32), shape((4, 256, 256), BF16), shape((4, 256, 256), BF16),
            shape((256, 512), BF16), shape((256, 512), BF16),
        ],
        in_specs=[pl.BlockSpec(memory_space=pl.ANY)] * 3,
        out_specs=[pl.BlockSpec(memory_space=pltpu.VMEM)] * 5,
        scratch_shapes=[
            vm((4096, 128), F32), vm((4, 256, 256), F32), vm((256, 256), F32),
            vm((256, 1024), BF16), vm((256, 1024), BF16),
            vm((2, 256, 256), F32), vm((2, 128, 256), F32), vm((2, 128, 256), F32),
            vm((2, 8, 16, 256), F32), vm((2, 256, 256), F32), vm((2, 8, 4, 16, 256), F32),
            vm((512, 256), F32), vm((256, 512), BF16), vm((256, 512), BF16),
            vm((16, 256), F32), vm((8, 16, 256), F32), vm((16, 256), F32),
            vm((4, 16, 256), F32), vm((256, 256), F32),
            dma((3,)), dma((7,)), dma((7,)), dma((8,)), dma((8,)),
            dma((2, 8)), dma((2, 8)), dma((2, 8)), dma((2, 8)),
            dma((2, 8)), dma((2, 8)), dma((8,)), dma((8,)),
            dma((2, 2, 8)), dma((2, 2, 8)), dma((2, 8)), dma((2, 8)), dma((4,)), dma((4,)),
        ],
        compiler_params=pltpu.CompilerParams(
            collective_id=0, has_side_effects=True, vmem_limit_bytes=VMEM_LIMIT
        ),
        name="band_update",
    )(*[pltpu.with_memory_space_constraint(arg, pltpu.HBM) for arg in (a, v, t_factor)])
    out = pl.pallas_call(
        finish_kernel,
        out_shape=shape((4096, 128), F32),
        in_specs=[pl.BlockSpec(memory_space=pltpu.VMEM)] * 5,
        out_specs=pl.BlockSpec(memory_space=pl.ANY),
        scratch_shapes=[vm((4096, 128), F32), dma((4,))],
        compiler_params=pltpu.CompilerParams(vmem_limit_bytes=VMEM_LIMIT // 2),
        name="band_finish",
    )(*parts)
    return out.reshape(matrix.shape)


def solution(mesh):
    in_specs = (P(None, "row", None, None, "col", None), P(None, "row", None, None), P())
    out_specs = P(None, "row", None, None, "col", None)
    return jax.shard_map(
        per_device, mesh=mesh, in_specs=in_specs, out_specs=out_specs, check_vma=False
    )
```

```python
import jax
import jax.numpy as jnp
from jax import lax
from jax.experimental import pallas as pl
from jax.experimental.pallas import tpu as pltpu
from jax.sharding import PartitionSpec as P

F32 = jnp.float32
BF16 = jnp.bfloat16
MESH = pl.DeviceIdType.MESH
NN = (((1,), (0,)), ((), ()))
NT = (((1,), (1,)), ((), ()))
Y, Z, X = 8, 8, 4
VMEM_LIMIT = 24 * 1024 * 1024


def rem(value, by):
    return lax.rem(value, jnp.int32(by))


def div(value, by):
    return lax.div(value, jnp.int32(by))


def split(value):
    high = value.astype(BF16)
    return high, (value - high.astype(F32)).astype(BF16)


def dot3(left, right, dims):
    def dot(a, b):
        return lax.dot_general(a, b, dims, preferred_element_type=F32)

    return dot(left[0], right[0]) + (dot(left[0], right[1]) + dot(left[1], right[0]))


def unit_lower(block):
    i = lax.broadcasted_iota(jnp.int32, block.shape, 0)
    k = lax.broadcasted_iota(jnp.int32, block.shape, 1)
    return jnp.where(i > k, block, jnp.where(i == k, 1.0, 0.0).astype(F32))


def kernel(
    a_hbm, v_hbm, t_hbm, o_s, uh, ul, wh, wl, a_s, v_s, t_s,
    vth, vtl, qt, xbuf, rsrc, rs, pct, prt, vc, uch, ucl, gsrc, gz, gsum, gx, gt,
    ld_sem, one_s, one_r, v_s_s, v_s_r, rs_s, rs_r, y_s, y_r,
    z_s, z_r, gz_s, gz_r, x_s, x_r, f_s, f_r, gx_s, gx_r,
):
    row = lax.axis_index("row")
    col = lax.axis_index("col")
    y, j = div(row, 2), rem(row, 2)
    z, x = div(col, X), rem(col, X)
    half, pos = div(col, 16), rem(col, 16)
    zs = [rem(z + Z - d, Z) for d in range(Z)]
    xs = [rem(x + d, X) for d in range(X)]
    ys = [rem(y + d, Y) for d in range(Y)]

    def flip(index):
        return index + 1 - 2 * rem(index, 2)

    def slice_at(position):
        other = flip(position)
        return 8 * rem(other, 2) + div(other, 2)

    mine, held = 8 * j + y, slice_at(pos)
    t_target, t_source = (pos, 16 * half + flip(row)), (flip(pos), 16 * half + row)
    partner = (2 * y + 1 - j, col)

    def y_peer(d):
        return (2 * ys[d] + j, col)

    def z_peer(d):
        return (row, X * zs[Z - d] + x)

    def x_peer(d):
        return (row, X * z + xs[d % X])

    def v_target(d):
        return (2 * rem(held + d, Y) + div(held, 8), 16 * half + row)

    def rows(start, size, step=16):
        return pl.ds(pl.multiple_of(start, step), size)

    started = []

    def send(src, dst, ssem, rsem, target):
        copy = pltpu.make_async_remote_copy(
            src_ref=src, dst_ref=dst, send_sem=ssem, recv_sem=rsem,
            device_id={"row": target[0], "col": target[1]}, device_id_type=MESH,
        )
        copy.start()
        started.append(copy)
        return copy

    loads = [
        pltpu.make_async_copy(src, dst, ld_sem.at[i])
        for i, (src, dst) in enumerate([(v_hbm, v_s), (a_hbm, a_s), (t_hbm, t_s)])
    ]
    for copy in loads:
        copy.start()
    barrier = pltpu.get_barrier_semaphore()
    greeted = (
        [y_peer(d) for d in range(1, Y)] + [z_peer(d) for d in range(1, Z)]
        + [x_peer(d) for d in range(1, X)] + [partner, t_source]
        + [(pos, 16 * half + 2 * i + 1 - j) for i in range(8)]
    )
    for peer in greeted:
        pl.semaphore_signal(
            barrier, inc=1, device_id={"row": peer[0], "col": peer[1]}, device_id_type=MESH
        )

    loads[0].wait()
    for lr in range(4):
        block = v_s[lr]
        if lr == 0:
            block = jnp.where(row == 0, unit_lower(block), block)
        high, low = split(block.T)
        vth[:, 256 * lr : 256 * lr + 256] = high
        vtl[:, 256 * lr : 256 * lr + 256] = low
        high, low = split(block)
        uh[lr] = high
        ul[lr] = low

    loads[1].wait()

    def partial(lc):
        block = jnp.concatenate(
            [a_s[pl.ds(2 * lc + q, 1024, stride=4), :] for q in range(2)], axis=1
        )
        qt[lc] = dot3((vth[...], vtl[...]), split(block), NN)

    def swap_of(lc):
        return send(
            qt.at[lc, rows(128 * (1 - j), 128)], xbuf.at[lc],
            one_s.at[lc], one_r.at[lc], partner,
        )

    order = (4, 3, 5, 2, 6, 1, 7)

    partial(0)
    pl.semaphore_wait(barrier, len(greeted))
    swaps = [swap_of(0)]
    v_part = v_s.at[half + 2 * div(held, 8), rows(32 * rem(held, 8), 32)]
    v_moves = [
        send(v_part, vc.at[rows(32 * held, 32)], v_s_s.at[d], v_s_r.at[d], v_target(d))
        for d in range(8)
    ]
    partial(1)
    swaps.append(swap_of(1))
    scatter = []
    for lc in range(2):
        swaps[lc].wait_recv()
        rsrc[lc] = qt[lc, rows(128 * j, 128), :] + xbuf[lc]
        scatter.append([
            send(
                rsrc.at[lc, rows(16 * ys[d], 16)], rs.at[lc, d],
                rs_s.at[lc, d], rs_r.at[lc, d], y_peer(d),
            )
            for d in order
        ])
    loads[2].wait()
    factor = split(t_s[...])
    for lr in range(4):
        high, low = split(dot3((uh[lr], ul[lr]), factor, NT))
        uh[lr] = high
        ul[lr] = low
    own = rows(16 * mine, 16)
    t_z, t_x = 4 * half + div(flip(row), X), rem(flip(row), X)
    totals, t_moves = [], []
    for lc in range(2):
        total = rsrc[lc, rows(16 * y, 16), :]
        for copy, d in zip(scatter[lc], order):
            copy.wait_recv()
            total = total + rs[lc, d]
        pct[lc, own, :] = total
        totals.append(total)
        t_moves.append(send(
            pct.at[lc, own], prt.at[lc, t_z, t_x], one_s.at[2 + lc], one_r.at[2 + lc], t_target
        ))
    for copy in v_moves:
        copy.wait_recv()
    v_half = vc.at[rows(256 * j, 256)]
    v_swap = send(v_half, v_half, one_s.at[4], one_r.at[4], partner)
    def x_send(d, lc):
        part = prt.at[lc, zs[d], x]
        return [
            send(part, part, x_s.at[side, lc, d], x_r.at[side, lc, d], x_peer(1 - 2 * side))
            for side in range(2)
        ]

    near = (1, 7, 2, 6, 3, 5, 4)
    z_gather, x_gather = [], [{}, {}]
    for lc in range(2):
        t_moves[lc].wait_recv()
        chunk = prt.at[lc, z, x]
        z_gather.append({
            d: send(chunk, chunk, z_s.at[lc, d], z_r.at[lc, d], z_peer(d)) for d in near
        })
        x_gather[lc][0] = x_send(0, lc)
    p_part = pct.at[:, own]
    p_gather = [
        send(p_part, p_part, y_s.at[0, d], y_r.at[0, d], y_peer(d)) for d in order
    ]
    v_swap.wait_recv()
    first = vc[0:256, :]
    first = jnp.where(col == 0, unit_lower(first), first)
    v_cols = [split(first), split(vc[256:512, :])]
    gsrc[...] = dot3(split(totals[0]), v_cols[0], NN) + dot3(split(totals[1]), v_cols[1], NN)
    g_z = [send(gsrc, gz.at[d], gz_s.at[d], gz_r.at[d], z_peer(d)) for d in order]
    for lc in range(2):
        high, low = split(dot3(factor, v_cols[lc], NT))
        uch[:, 256 * lc : 256 * lc + 256] = high
        ucl[:, 256 * lc : 256 * lc + 256] = low

    forward = [[], []]

    def pass_on(d, lc):
        x_gather[lc][d][lc].wait_recv()
        part = prt.at[lc, zs[d], xs[3 - 2 * lc]]
        forward[lc].append(
            send(part, part, f_s.at[lc, d], f_r.at[lc, d], x_peer(1 - 2 * lc))
        )

    for d in near:
        z_gather[0][d].wait_recv()
        x_gather[0][d] = x_send(d, 0)
    for d, e in zip(near, (0,) + near):
        z_gather[1][d].wait_recv()
        x_gather[1][d] = x_send(d, 1)
        pass_on(e, 0)
    part_sum = gsrc[...]
    for copy, d in zip(g_z, order):
        copy.wait_recv()
        part_sum = part_sum + gz[d]
    gsum[...] = part_sum
    g_x = [
        send(gsum, gx.at[d], gx_s.at[d], gx_r.at[d], x_peer(d)) for d in range(1, X)
    ]
    pass_on(near[-1], 0)
    for d in (0,) + near:
        pass_on(d, 1)
    for d, copy in zip(range(1, X), g_x):
        copy.wait_recv()
        part_sum = part_sum + gx[d]
    gt[own, :] = part_sum
    g_gather = [
        send(gt.at[own], gt.at[own], y_s.at[1, d], y_r.at[1, d], y_peer(d)) for d in order
    ]
    for copy in p_gather:
        copy.wait_recv()
    p_half = pct.at[:, rows(128 * j, 128)]
    p_swap = send(p_half, p_half, one_s.at[5], one_r.at[5], partner)

    places = [(2 * (e % 8) + e // 8) ^ 1 for e in range(16)]
    for lc in range(2):
        for d in (0,) + near:
            x_gather[lc][d][1 - lc].wait_recv()
        for copy in forward[lc]:
            copy.wait_recv()
        for h in range(2):
            lr = h + 2 * lc
            left = split(jnp.concatenate(
                [prt[lc, 4 * h + p // X, p % X] for p in places], axis=0
            ).T)
            for oc in range(2):
                cols = slice(256 * oc, 256 * oc + 256)
                delta = dot3(left, (uch[:, cols], ucl[:, cols]), NN)
                for q in range(2):
                    where = pl.ds(lr * 1024 + 2 * oc + q, 256, stride=4)
                    o_s[where, :] = a_s[where, :] - delta[:, 128 * q : 128 * q + 128]
    for copy in g_gather:
        copy.wait_recv()
    g_half = gt.at[rows(128 * j, 128)]
    g_swap = send(g_half, g_half, one_s.at[6], one_r.at[6], partner)
    p_swap.wait_recv()
    g_swap.wait_recv()
    inner = split(gt[...])
    for lc in range(2):
        cols = slice(256 * lc, 256 * lc + 256)
        high, low = split(pct[lc] - dot3(inner, (uch[:, cols], ucl[:, cols]), NN))
        wh[:, cols] = high
        wl[:, cols] = low
    for copy in started:
        copy.wait_send()


def finish_kernel(o_ref, uh_ref, ul_ref, wh_ref, wl_ref, out_hbm, buf, sems):
    def store(lr):
        part = pl.ds(1024 * lr, 1024)
        return pltpu.make_async_copy(buf.at[part], out_hbm.at[part], sems.at[lr])

    right = [
        (wh_ref[:, 256 * oc : 256 * oc + 256], wl_ref[:, 256 * oc : 256 * oc + 256])
        for oc in range(2)
    ]
    for lr in range(4):
        left = (uh_ref[lr], ul_ref[lr])
        for oc in range(2):
            delta = dot3(left, right[oc], NN)
            for q in range(2):
                where = pl.ds(1024 * lr + 2 * oc + q, 256, stride=4)
                buf[where, :] = o_ref[where, :] - delta[:, 128 * q : 128 * q + 128]
        store(lr).start()
    for lr in range(4):
        store(lr).wait()


def per_device(matrix, vectors, t_factor):
    a = matrix.reshape(4096, 128)
    v = vectors.reshape(4, 256, 256)
    vm = pltpu.VMEM
    dma = pltpu.SemaphoreType.DMA
    shape = jax.ShapeDtypeStruct
    parts = pl.pallas_call(
        kernel,
        out_shape=[
            shape((4096, 128), F32), shape((4, 256, 256), BF16), shape((4, 256, 256), BF16),
            shape((256, 512), BF16), shape((256, 512), BF16),
        ],
        in_specs=[pl.BlockSpec(memory_space=pl.ANY)] * 3,
        out_specs=[pl.BlockSpec(memory_space=pltpu.VMEM)] * 5,
        scratch_shapes=[
            vm((4096, 128), F32), vm((4, 256, 256), F32), vm((256, 256), F32),
            vm((256, 1024), BF16), vm((256, 1024), BF16),
            vm((2, 256, 256), F32), vm((2, 128, 256), F32), vm((2, 128, 256), F32),
            vm((2, 8, 16, 256), F32), vm((2, 256, 256), F32), vm((2, 8, 4, 16, 256), F32),
            vm((512, 256), F32), vm((256, 512), BF16), vm((256, 512), BF16),
            vm((16, 256), F32), vm((8, 16, 256), F32), vm((16, 256), F32),
            vm((4, 16, 256), F32), vm((256, 256), F32),
            dma((3,)), dma((7,)), dma((7,)), dma((8,)), dma((8,)),
            dma((2, 8)), dma((2, 8)), dma((2, 8)), dma((2, 8)),
            dma((2, 8)), dma((2, 8)), dma((8,)), dma((8,)),
            dma((2, 2, 8)), dma((2, 2, 8)), dma((2, 8)), dma((2, 8)), dma((4,)), dma((4,)),
        ],
        compiler_params=pltpu.CompilerParams(
            collective_id=0, has_side_effects=True, vmem_limit_bytes=VMEM_LIMIT
        ),
        name="band_update",
    )(*[pltpu.with_memory_space_constraint(arg, pltpu.HBM) for arg in (a, v, t_factor)])
    out = pl.pallas_call(
        finish_kernel,
        out_shape=shape((4096, 128), F32),
        in_specs=[pl.BlockSpec(memory_space=pltpu.VMEM)] * 5,
        out_specs=pl.BlockSpec(memory_space=pl.ANY),
        scratch_shapes=[vm((4096, 128), F32), dma((4,))],
        compiler_params=pltpu.CompilerParams(vmem_limit_bytes=VMEM_LIMIT // 2),
        name="band_finish",
    )(*parts)
    return out.reshape(matrix.shape)


def solution(mesh):
    in_specs = (P(None, "row", None, None, "col", None), P(None, "row", None, None), P())
    out_specs = P(None, "row", None, None, "col", None)
    return jax.shard_map(
        per_device, mesh=mesh, in_specs=in_specs, out_specs=out_specs, check_vma=False
    )
```

```python
import jax
import jax.numpy as jnp
from jax import lax
from jax.experimental import pallas as pl
from jax.experimental.pallas import tpu as pltpu
from jax.sharding import PartitionSpec as P

F32 = jnp.float32
BF16 = jnp.bfloat16
MESH = pl.DeviceIdType.MESH
NN = (((1,), (0,)), ((), ()))
NT = (((1,), (1,)), ((), ()))
Y, Z, X = 8, 8, 4
VMEM_LIMIT = 24 * 1024 * 1024


def rem(value, by):
    return lax.rem(value, jnp.int32(by))


def div(value, by):
    return lax.div(value, jnp.int32(by))


def split(value):
    high = value.astype(BF16)
    return high, (value - high.astype(F32)).astype(BF16)


def dot3(left, right, dims):
    def dot(a, b):
        return lax.dot_general(a, b, dims, preferred_element_type=F32)

    return dot(left[0], right[0]) + (dot(left[0], right[1]) + dot(left[1], right[0]))


def unit_lower(block):
    i = lax.broadcasted_iota(jnp.int32, block.shape, 0)
    k = lax.broadcasted_iota(jnp.int32, block.shape, 1)
    return jnp.where(i > k, block, jnp.where(i == k, 1.0, 0.0).astype(F32))


def kernel(
    a_hbm, v_hbm, t_hbm, o_s, uh, ul, wh, wl, a_s, v_s, t_s,
    vth, vtl, qt, xbuf, rsrc, rs, pct, prt, vc, uch, ucl, gsrc, gz, gsum, gx, gt,
    ld_sem, one_s, one_r, v_s_s, v_s_r, rs_s, rs_r, y_s, y_r,
    z_s, z_r, gz_s, gz_r, x_s, x_r, f_s, f_r, gx_s, gx_r,
):
    row = lax.axis_index("row")
    col = lax.axis_index("col")
    y, j = div(row, 2), rem(row, 2)
    z, x = div(col, X), rem(col, X)
    half, pos = div(col, 16), rem(col, 16)
    zs = [rem(z + Z - d, Z) for d in range(Z)]
    xs = [rem(x + d, X) for d in range(X)]
    ys = [rem(y + d, Y) for d in range(Y)]

    def flip(index):
        return index + 1 - 2 * rem(index, 2)

    def slice_at(position):
        other = flip(position)
        return 8 * rem(other, 2) + div(other, 2)

    mine, held = 8 * j + y, slice_at(pos)
    t_target, t_source = (pos, 16 * half + flip(row)), (flip(pos), 16 * half + row)
    partner = (2 * y + 1 - j, col)

    def y_peer(d):
        return (2 * ys[d] + j, col)

    def z_peer(d):
        return (row, X * zs[Z - d] + x)

    def x_peer(d):
        return (row, X * z + xs[d % X])

    def v_target(d):
        return (2 * rem(held + d, Y) + div(held, 8), 16 * half + row)

    def rows(start, size, step=16):
        return pl.ds(pl.multiple_of(start, step), size)

    started = []

    def send(src, dst, ssem, rsem, target):
        copy = pltpu.make_async_remote_copy(
            src_ref=src, dst_ref=dst, send_sem=ssem, recv_sem=rsem,
            device_id={"row": target[0], "col": target[1]}, device_id_type=MESH,
        )
        copy.start()
        started.append(copy)
        return copy

    loads = [
        pltpu.make_async_copy(src, dst, ld_sem.at[i])
        for i, (src, dst) in enumerate([(v_hbm, v_s), (a_hbm, a_s), (t_hbm, t_s)])
    ]
    for copy in loads:
        copy.start()
    barrier = pltpu.get_barrier_semaphore()
    greeted = (
        [y_peer(d) for d in range(1, Y)] + [z_peer(d) for d in range(1, Z)]
        + [x_peer(d) for d in range(1, X)] + [partner, t_source]
        + [(pos, 16 * half + 2 * i + 1 - j) for i in range(8)]
    )
    for peer in greeted:
        pl.semaphore_signal(
            barrier, inc=1, device_id={"row": peer[0], "col": peer[1]}, device_id_type=MESH
        )

    loads[0].wait()
    for lr in range(4):
        block = v_s[lr]
        if lr == 0:
            block = jnp.where(row == 0, unit_lower(block), block)
        high, low = split(block.T)
        vth[:, 256 * lr : 256 * lr + 256] = high
        vtl[:, 256 * lr : 256 * lr + 256] = low
        high, low = split(block)
        uh[lr] = high
        ul[lr] = low

    loads[1].wait()

    def partial(lc):
        block = jnp.concatenate(
            [a_s[pl.ds(2 * lc + q, 1024, stride=4), :] for q in range(2)], axis=1
        )
        qt[lc] = dot3((vth[...], vtl[...]), split(block), NN)

    def swap_of(lc):
        return send(
            qt.at[lc, rows(128 * (1 - j), 128)], xbuf.at[lc],
            one_s.at[lc], one_r.at[lc], partner,
        )

    order = (4, 3, 5, 2, 6, 1, 7)

    partial(0)
    pl.semaphore_wait(barrier, len(greeted))
    swaps = [swap_of(0)]
    v_part = v_s.at[half + 2 * div(held, 8), rows(32 * rem(held, 8), 32)]
    v_moves = [
        send(v_part, vc.at[rows(32 * held, 32)], v_s_s.at[d], v_s_r.at[d], v_target(d))
        for d in range(8)
    ]
    partial(1)
    swaps.append(swap_of(1))
    scatter = []
    for lc in range(2):
        swaps[lc].wait_recv()
        rsrc[lc] = qt[lc, rows(128 * j, 128), :] + xbuf[lc]
        scatter.append([
            send(
                rsrc.at[lc, rows(16 * ys[d], 16)], rs.at[lc, d],
                rs_s.at[lc, d], rs_r.at[lc, d], y_peer(d),
            )
            for d in order
        ])
    loads[2].wait()
    factor = split(t_s[...])
    for lr in range(4):
        high, low = split(dot3((uh[lr], ul[lr]), factor, NT))
        uh[lr] = high
        ul[lr] = low
    for copy in v_moves:
        copy.wait_recv()
    v_half = vc.at[rows(256 * j, 256)]
    v_swap = send(v_half, v_half, one_s.at[4], one_r.at[4], partner)
    own = rows(16 * mine, 16)
    t_z, t_x = 4 * half + div(flip(row), X), rem(flip(row), X)
    totals, t_moves = [], []
    for lc in range(2):
        total = rsrc[lc, rows(16 * y, 16), :]
        for copy, d in zip(scatter[lc], order):
            copy.wait_recv()
            total = total + rs[lc, d]
        pct[lc, own, :] = total
        totals.append(total)
        t_moves.append(send(
            pct.at[lc, own], prt.at[lc, t_z, t_x], one_s.at[2 + lc], one_r.at[2 + lc], t_target
        ))
    v_swap.wait_recv()
    first = vc[0:256, :]
    first = jnp.where(col == 0, unit_lower(first), first)
    v_cols = [split(first), split(vc[256:512, :])]
    gsrc[...] = dot3(split(totals[0]), v_cols[0], NN) + dot3(split(totals[1]), v_cols[1], NN)
    g_z = [send(gsrc, gz.at[d], gz_s.at[d], gz_r.at[d], z_peer(d)) for d in order]
    p_part = pct.at[:, own]
    p_gather = [
        send(p_part, p_part, y_s.at[0, d], y_r.at[0, d], y_peer(d)) for d in order
    ]
    for lc in range(2):
        high, low = split(dot3(factor, v_cols[lc], NT))
        uch[:, 256 * lc : 256 * lc + 256] = high
        ucl[:, 256 * lc : 256 * lc + 256] = low

    def x_send(d, lc):
        part = prt.at[lc, zs[d], x]
        return [
            send(part, part, x_s.at[side, lc, d], x_r.at[side, lc, d], x_peer(1 - 2 * side))
            for side in range(2)
        ]

    near = (1, 7, 2, 6, 3, 5, 4)
    z_gather, x_gather = [], [{}, {}]
    for lc in range(2):
        t_moves[lc].wait_recv()
        chunk = prt.at[lc, z, x]
        z_gather.append({
            d: send(chunk, chunk, z_s.at[lc, d], z_r.at[lc, d], z_peer(d)) for d in near
        })
        x_gather[lc][0] = x_send(0, lc)
    part_sum = gsrc[...]
    for copy, d in zip(g_z, order):
        copy.wait_recv()
        part_sum = part_sum + gz[d]
    gsum[...] = part_sum
    g_x = [
        send(gsum, gx.at[d], gx_s.at[d], gx_r.at[d], x_peer(d)) for d in range(1, X)
    ]

    forward = [[], []]

    def pass_on(d, lc):
        x_gather[lc][d][lc].wait_recv()
        part = prt.at[lc, zs[d], xs[3 - 2 * lc]]
        forward[lc].append(
            send(part, part, f_s.at[lc, d], f_r.at[lc, d], x_peer(1 - 2 * lc))
        )

    for d in near:
        z_gather[0][d].wait_recv()
        x_gather[0][d] = x_send(d, 0)
    for d, copy in zip(range(1, X), g_x):
        copy.wait_recv()
        part_sum = part_sum + gx[d]
    gt[own, :] = part_sum
    g_gather = [
        send(gt.at[own], gt.at[own], y_s.at[1, d], y_r.at[1, d], y_peer(d)) for d in order
    ]
    for d, e in zip(near, (0,) + near):
        z_gather[1][d].wait_recv()
        x_gather[1][d] = x_send(d, 1)
        pass_on(e, 0)
    pass_on(near[-1], 0)
    for d in (0,) + near:
        pass_on(d, 1)
    for copy in p_gather:
        copy.wait_recv()
    p_half = pct.at[:, rows(128 * j, 128)]
    p_swap = send(p_half, p_half, one_s.at[5], one_r.at[5], partner)

    for copy in g_gather:
        copy.wait_recv()
    g_half = gt.at[rows(128 * j, 128)]
    g_swap = send(g_half, g_half, one_s.at[6], one_r.at[6], partner)
    places = [(2 * (e % 8) + e // 8) ^ 1 for e in range(16)]
    for lc in range(2):
        for d in (0,) + near:
            x_gather[lc][d][1 - lc].wait_recv()
        for copy in forward[lc]:
            copy.wait_recv()
        for h in range(2):
            lr = h + 2 * lc
            left = split(jnp.concatenate(
                [prt[lc, 4 * h + p // X, p % X] for p in places], axis=0
            ).T)
            for oc in range(2):
                cols = slice(256 * oc, 256 * oc + 256)
                delta = dot3(left, (uch[:, cols], ucl[:, cols]), NN)
                for q in range(2):
                    where = pl.ds(lr * 1024 + 2 * oc + q, 256, stride=4)
                    o_s[where, :] = a_s[where, :] - delta[:, 128 * q : 128 * q + 128]
    p_swap.wait_recv()
    g_swap.wait_recv()
    inner = split(gt[...])
    for lc in range(2):
        cols = slice(256 * lc, 256 * lc + 256)
        high, low = split(pct[lc] - dot3(inner, (uch[:, cols], ucl[:, cols]), NN))
        wh[:, cols] = high
        wl[:, cols] = low
    for copy in started:
        copy.wait_send()


def finish_kernel(o_ref, uh_ref, ul_ref, wh_ref, wl_ref, out_hbm, buf, sems):
    def store(lr):
        part = pl.ds(1024 * lr, 1024)
        return pltpu.make_async_copy(buf.at[part], out_hbm.at[part], sems.at[lr])

    right = [
        (wh_ref[:, 256 * oc : 256 * oc + 256], wl_ref[:, 256 * oc : 256 * oc + 256])
        for oc in range(2)
    ]
    for lr in range(4):
        left = (uh_ref[lr], ul_ref[lr])
        for oc in range(2):
            delta = dot3(left, right[oc], NN)
            for q in range(2):
                where = pl.ds(1024 * lr + 2 * oc + q, 256, stride=4)
                buf[where, :] = o_ref[where, :] - delta[:, 128 * q : 128 * q + 128]
        store(lr).start()
    for lr in range(4):
        store(lr).wait()


def per_device(matrix, vectors, t_factor):
    a = matrix.reshape(4096, 128)
    v = vectors.reshape(4, 256, 256)
    vm = pltpu.VMEM
    dma = pltpu.SemaphoreType.DMA
    shape = jax.ShapeDtypeStruct
    parts = pl.pallas_call(
        kernel,
        out_shape=[
            shape((4096, 128), F32), shape((4, 256, 256), BF16), shape((4, 256, 256), BF16),
            shape((256, 512), BF16), shape((256, 512), BF16),
        ],
        in_specs=[pl.BlockSpec(memory_space=pl.ANY)] * 3,
        out_specs=[pl.BlockSpec(memory_space=pltpu.VMEM)] * 5,
        scratch_shapes=[
            vm((4096, 128), F32), vm((4, 256, 256), F32), vm((256, 256), F32),
            vm((256, 1024), BF16), vm((256, 1024), BF16),
            vm((2, 256, 256), F32), vm((2, 128, 256), F32), vm((2, 128, 256), F32),
            vm((2, 8, 16, 256), F32), vm((2, 256, 256), F32), vm((2, 8, 4, 16, 256), F32),
            vm((512, 256), F32), vm((256, 512), BF16), vm((256, 512), BF16),
            vm((16, 256), F32), vm((8, 16, 256), F32), vm((16, 256), F32),
            vm((4, 16, 256), F32), vm((256, 256), F32),
            dma((3,)), dma((7,)), dma((7,)), dma((8,)), dma((8,)),
            dma((2, 8)), dma((2, 8)), dma((2, 8)), dma((2, 8)),
            dma((2, 8)), dma((2, 8)), dma((8,)), dma((8,)),
            dma((2, 2, 8)), dma((2, 2, 8)), dma((2, 8)), dma((2, 8)), dma((4,)), dma((4,)),
        ],
        compiler_params=pltpu.CompilerParams(
            collective_id=0, has_side_effects=True, vmem_limit_bytes=VMEM_LIMIT
        ),
        name="band_update",
    )(*[pltpu.with_memory_space_constraint(arg, pltpu.HBM) for arg in (a, v, t_factor)])
    out = pl.pallas_call(
        finish_kernel,
        out_shape=shape((4096, 128), F32),
        in_specs=[pl.BlockSpec(memory_space=pltpu.VMEM)] * 5,
        out_specs=pl.BlockSpec(memory_space=pl.ANY),
        scratch_shapes=[vm((4096, 128), F32), dma((4,))],
        compiler_params=pltpu.CompilerParams(vmem_limit_bytes=VMEM_LIMIT // 2),
        name="band_finish",
    )(*parts)
    return out.reshape(matrix.shape)


def solution(mesh):
    in_specs = (P(None, "row", None, None, "col", None), P(None, "row", None, None), P())
    out_specs = P(None, "row", None, None, "col", None)
    return jax.shard_map(
        per_device, mesh=mesh, in_specs=in_specs, out_specs=out_specs, check_vma=False
    )
```

```python
import jax
import jax.numpy as jnp
from jax import lax
from jax.experimental import pallas as pl
from jax.experimental.pallas import tpu as pltpu
from jax.sharding import PartitionSpec as P

F32 = jnp.float32
BF16 = jnp.bfloat16
MESH = pl.DeviceIdType.MESH
NN = (((1,), (0,)), ((), ()))
NT = (((1,), (1,)), ((), ()))
Y, Z, X = 8, 8, 4
VMEM_LIMIT = 24 * 1024 * 1024


def rem(value, by):
    return lax.rem(value, jnp.int32(by))


def div(value, by):
    return lax.div(value, jnp.int32(by))


def split(value):
    high = value.astype(BF16)
    return high, (value - high.astype(F32)).astype(BF16)


def dot3(left, right, dims):
    def dot(a, b):
        return lax.dot_general(a, b, dims, preferred_element_type=F32)

    return dot(left[0], right[0]) + (dot(left[0], right[1]) + dot(left[1], right[0]))


def unit_lower(block):
    i = lax.broadcasted_iota(jnp.int32, block.shape, 0)
    k = lax.broadcasted_iota(jnp.int32, block.shape, 1)
    return jnp.where(i > k, block, jnp.where(i == k, 1.0, 0.0).astype(F32))


def kernel(
    a_hbm, v_hbm, t_hbm, o_s, uh, ul, wh, wl, a_s, v_s, t_s,
    vth, vtl, qt, xbuf, rsrc, rs, cmb, pct, prt, vc, uch, ucl, gsrc, gz, gsum, gx, gt,
    ld_sem, one_s, one_r, v_s_s, v_s_r, rs_s, rs_r, y_s, y_r,
    z_s, z_r, gz_s, gz_r, x_s, x_r, f_s, f_r, gx_s, gx_r,
):
    row = lax.axis_index("row")
    col = lax.axis_index("col")
    y, j = div(row, 2), rem(row, 2)
    z, x = div(col, X), rem(col, X)
    half, pos = div(col, 16), rem(col, 16)
    zs = [rem(z + Z - d, Z) for d in range(Z)]
    xs = [rem(x + d, X) for d in range(X)]
    ys = [rem(y + d, Y) for d in range(Y)]

    def flip(index):
        return index + 1 - 2 * rem(index, 2)

    def slice_at(position):
        other = flip(position)
        return 8 * rem(other, 2) + div(other, 2)

    mine, held = 8 * j + y, slice_at(pos)
    t_target, t_source = (pos, 16 * half + flip(row)), (flip(pos), 16 * half + row)
    partner = (2 * y + 1 - j, col)

    def y_peer(d):
        return (2 * ys[d] + j, col)

    def z_peer(d):
        return (row, X * zs[Z - d] + x)

    def x_peer(d):
        return (row, X * z + xs[d % X])

    def v_target(d):
        return (2 * rem(held + d, Y) + div(held, 8), 16 * half + row)

    def rows(start, size, step=16):
        return pl.ds(pl.multiple_of(start, step), size)

    started = []

    def send(src, dst, ssem, rsem, target):
        copy = pltpu.make_async_remote_copy(
            src_ref=src, dst_ref=dst, send_sem=ssem, recv_sem=rsem,
            device_id={"row": target[0], "col": target[1]}, device_id_type=MESH,
        )
        copy.start()
        started.append(copy)
        return copy

    loads = [
        pltpu.make_async_copy(src, dst, ld_sem.at[i])
        for i, (src, dst) in enumerate([(v_hbm, v_s), (a_hbm, a_s), (t_hbm, t_s)])
    ]
    for copy in loads:
        copy.start()
    barrier = pltpu.get_barrier_semaphore()
    greeted = (
        [y_peer(d) for d in range(1, Y)] + [z_peer(d) for d in range(1, Z)]
        + [x_peer(d) for d in range(1, X)] + [partner, t_source]
        + [(pos, 16 * half + 2 * i + 1 - j) for i in range(8)]
    )
    for peer in greeted:
        pl.semaphore_signal(
            barrier, inc=1, device_id={"row": peer[0], "col": peer[1]}, device_id_type=MESH
        )

    loads[0].wait()
    for lr in range(4):
        block = v_s[lr]
        if lr == 0:
            block = jnp.where(row == 0, unit_lower(block), block)
        high, low = split(block.T)
        vth[:, 256 * lr : 256 * lr + 256] = high
        vtl[:, 256 * lr : 256 * lr + 256] = low
        high, low = split(block)
        uh[lr] = high
        ul[lr] = low

    loads[1].wait()

    def partial(lc):
        block = jnp.concatenate(
            [a_s[pl.ds(2 * lc + q, 1024, stride=4), :] for q in range(2)], axis=1
        )
        qt[lc] = dot3((vth[...], vtl[...]), split(block), NN)

    def swap_of(lc):
        return send(
            qt.at[lc, rows(128 * (1 - j), 128)], xbuf.at[lc],
            one_s.at[lc], one_r.at[lc], partner,
        )

    order = (4, 3, 5, 2, 6, 1, 7)

    partial(0)
    pl.semaphore_wait(barrier, len(greeted))
    swaps = [swap_of(0)]
    v_part = v_s.at[half + 2 * div(held, 8), rows(32 * rem(held, 8), 32)]
    v_moves = [
        send(v_part, vc.at[rows(32 * held, 32)], v_s_s.at[d], v_s_r.at[d], v_target(d))
        for d in range(8)
    ]
    partial(1)
    swaps.append(swap_of(1))
    def own_part(lc, d):
        return rsrc[lc, rows(16 * ys[d % Y], 16), :]

    def scatter(lc, slot, src, d):
        hops[lc][slot] = send(
            src, rs.at[lc, slot], rs_s.at[lc, slot], rs_r.at[lc, slot], y_peer(d)
        )

    def add_and_pass(lc, arrived, chunk, slot, d):
        hops[lc][arrived].wait_recv()
        part = cmb.at[lc, slot - 4]
        part[...] = own_part(lc, chunk) + rs[lc, arrived]
        scatter(lc, slot, part, d)

    hops = [{}, {}]
    for lc in range(2):
        swaps[lc].wait_recv()
        rsrc[lc] = qt[lc, rows(128 * j, 128), :] + xbuf[lc]
        for slot, chunk, d in ((0, -4, 7), (1, 3, 1), (2, -1, 7), (3, 1, 1)):
            scatter(lc, slot, rsrc.at[lc, rows(16 * ys[chunk % Y], 16)], d)
    loads[2].wait()
    factor = split(t_s[...])
    for lr in range(4):
        high, low = split(dot3((uh[lr], ul[lr]), factor, NT))
        uh[lr] = high
        ul[lr] = low
    own = rows(16 * mine, 16)
    t_z, t_x = 4 * half + div(flip(row), X), rem(flip(row), X)
    for lc in range(2):
        add_and_pass(lc, 0, -3, 4, 7)
        add_and_pass(lc, 1, 2, 5, 2)
    for lc in range(2):
        add_and_pass(lc, 4, -2, 6, 6)
    totals, t_moves = [], []
    for lc in range(2):
        total = own_part(lc, 0)
        for slot in (2, 3, 5, 6):
            hops[lc][slot].wait_recv()
            total = total + rs[lc, slot]
        pct[lc, own, :] = total
        totals.append(total)
        t_moves.append(send(
            pct.at[lc, own], prt.at[lc, t_z, t_x], one_s.at[2 + lc], one_r.at[2 + lc], t_target
        ))
    for copy in v_moves:
        copy.wait_recv()
    v_half = vc.at[rows(256 * j, 256)]
    v_swap = send(v_half, v_half, one_s.at[4], one_r.at[4], partner)
    v_swap.wait_recv()
    first = vc[0:256, :]
    first = jnp.where(col == 0, unit_lower(first), first)
    v_cols = [split(first), split(vc[256:512, :])]
    gsrc[...] = dot3(split(totals[0]), v_cols[0], NN) + dot3(split(totals[1]), v_cols[1], NN)
    g_z = [send(gsrc, gz.at[d], gz_s.at[d], gz_r.at[d], z_peer(d)) for d in order]
    p_part = pct.at[:, own]
    p_gather = [
        send(p_part, p_part, y_s.at[0, d], y_r.at[0, d], y_peer(d)) for d in order
    ]
    for lc in range(2):
        high, low = split(dot3(factor, v_cols[lc], NT))
        uch[:, 256 * lc : 256 * lc + 256] = high
        ucl[:, 256 * lc : 256 * lc + 256] = low

    def x_send(d, lc):
        part = prt.at[lc, zs[d], x]
        return [
            send(part, part, x_s.at[side, lc, d], x_r.at[side, lc, d], x_peer(1 - 2 * side))
            for side in range(2)
        ]

    near = (1, 7, 2, 6, 3, 5, 4)
    z_gather, x_gather = [], [{}, {}]
    for lc in range(2):
        t_moves[lc].wait_recv()
        chunk = prt.at[lc, z, x]
        z_gather.append({
            d: send(chunk, chunk, z_s.at[lc, d], z_r.at[lc, d], z_peer(d)) for d in near
        })
        x_gather[lc][0] = x_send(0, lc)
    part_sum = gsrc[...]
    for copy, d in zip(g_z, order):
        copy.wait_recv()
        part_sum = part_sum + gz[d]
    gsum[...] = part_sum
    g_x = [
        send(gsum, gx.at[d], gx_s.at[d], gx_r.at[d], x_peer(d)) for d in range(1, X)
    ]

    forward = [[], []]

    def pass_on(d, lc):
        x_gather[lc][d][lc].wait_recv()
        part = prt.at[lc, zs[d], xs[3 - 2 * lc]]
        forward[lc].append(
            send(part, part, f_s.at[lc, d], f_r.at[lc, d], x_peer(1 - 2 * lc))
        )

    for d in near:
        z_gather[0][d].wait_recv()
        x_gather[0][d] = x_send(d, 0)
    for d, copy in zip(range(1, X), g_x):
        copy.wait_recv()
        part_sum = part_sum + gx[d]
    gt[own, :] = part_sum
    g_gather = [
        send(gt.at[own], gt.at[own], y_s.at[1, d], y_r.at[1, d], y_peer(d)) for d in order
    ]
    for d, e in zip(near, (0,) + near):
        z_gather[1][d].wait_recv()
        x_gather[1][d] = x_send(d, 1)
        pass_on(e, 0)
    pass_on(near[-1], 0)
    for d in (0,) + near:
        pass_on(d, 1)
    for copy in p_gather:
        copy.wait_recv()
    p_half = pct.at[:, rows(128 * j, 128)]
    p_swap = send(p_half, p_half, one_s.at[5], one_r.at[5], partner)

    for copy in g_gather:
        copy.wait_recv()
    g_half = gt.at[rows(128 * j, 128)]
    g_swap = send(g_half, g_half, one_s.at[6], one_r.at[6], partner)
    places = [(2 * (e % 8) + e // 8) ^ 1 for e in range(16)]
    for lc in range(2):
        for d in (0,) + near:
            x_gather[lc][d][1 - lc].wait_recv()
        for copy in forward[lc]:
            copy.wait_recv()
        for h in range(2):
            lr = h + 2 * lc
            left = split(jnp.concatenate(
                [prt[lc, 4 * h + p // X, p % X] for p in places], axis=0
            ).T)
            for oc in range(2):
                cols = slice(256 * oc, 256 * oc + 256)
                delta = dot3(left, (uch[:, cols], ucl[:, cols]), NN)
                for q in range(2):
                    where = pl.ds(lr * 1024 + 2 * oc + q, 256, stride=4)
                    o_s[where, :] = a_s[where, :] - delta[:, 128 * q : 128 * q + 128]
    p_swap.wait_recv()
    g_swap.wait_recv()
    inner = split(gt[...])
    for lc in range(2):
        cols = slice(256 * lc, 256 * lc + 256)
        high, low = split(pct[lc] - dot3(inner, (uch[:, cols], ucl[:, cols]), NN))
        wh[:, cols] = high
        wl[:, cols] = low
    for copy in started:
        copy.wait_send()


def finish_kernel(o_ref, uh_ref, ul_ref, wh_ref, wl_ref, out_hbm, buf, sems):
    def store(lr):
        part = pl.ds(1024 * lr, 1024)
        return pltpu.make_async_copy(buf.at[part], out_hbm.at[part], sems.at[lr])

    right = [
        (wh_ref[:, 256 * oc : 256 * oc + 256], wl_ref[:, 256 * oc : 256 * oc + 256])
        for oc in range(2)
    ]
    for lr in range(4):
        left = (uh_ref[lr], ul_ref[lr])
        for oc in range(2):
            delta = dot3(left, right[oc], NN)
            for q in range(2):
                where = pl.ds(1024 * lr + 2 * oc + q, 256, stride=4)
                buf[where, :] = o_ref[where, :] - delta[:, 128 * q : 128 * q + 128]
        store(lr).start()
    for lr in range(4):
        store(lr).wait()


def per_device(matrix, vectors, t_factor):
    a = matrix.reshape(4096, 128)
    v = vectors.reshape(4, 256, 256)
    vm = pltpu.VMEM
    dma = pltpu.SemaphoreType.DMA
    shape = jax.ShapeDtypeStruct
    parts = pl.pallas_call(
        kernel,
        out_shape=[
            shape((4096, 128), F32), shape((4, 256, 256), BF16), shape((4, 256, 256), BF16),
            shape((256, 512), BF16), shape((256, 512), BF16),
        ],
        in_specs=[pl.BlockSpec(memory_space=pl.ANY)] * 3,
        out_specs=[pl.BlockSpec(memory_space=pltpu.VMEM)] * 5,
        scratch_shapes=[
            vm((4096, 128), F32), vm((4, 256, 256), F32), vm((256, 256), F32),
            vm((256, 1024), BF16), vm((256, 1024), BF16),
            vm((2, 256, 256), F32), vm((2, 128, 256), F32), vm((2, 128, 256), F32),
            vm((2, 8, 16, 256), F32), vm((2, 3, 16, 256), F32), vm((2, 256, 256), F32), vm((2, 8, 4, 16, 256), F32),
            vm((512, 256), F32), vm((256, 512), BF16), vm((256, 512), BF16),
            vm((16, 256), F32), vm((8, 16, 256), F32), vm((16, 256), F32),
            vm((4, 16, 256), F32), vm((256, 256), F32),
            dma((3,)), dma((7,)), dma((7,)), dma((8,)), dma((8,)),
            dma((2, 8)), dma((2, 8)), dma((2, 8)), dma((2, 8)),
            dma((2, 8)), dma((2, 8)), dma((8,)), dma((8,)),
            dma((2, 2, 8)), dma((2, 2, 8)), dma((2, 8)), dma((2, 8)), dma((4,)), dma((4,)),
        ],
        compiler_params=pltpu.CompilerParams(
            collective_id=0, has_side_effects=True, vmem_limit_bytes=VMEM_LIMIT
        ),
        name="band_update",
    )(*[pltpu.with_memory_space_constraint(arg, pltpu.HBM) for arg in (a, v, t_factor)])
    out = pl.pallas_call(
        finish_kernel,
        out_shape=shape((4096, 128), F32),
        in_specs=[pl.BlockSpec(memory_space=pltpu.VMEM)] * 5,
        out_specs=pl.BlockSpec(memory_space=pl.ANY),
        scratch_shapes=[vm((4096, 128), F32), dma((4,))],
        compiler_params=pltpu.CompilerParams(vmem_limit_bytes=VMEM_LIMIT // 2),
        name="band_finish",
    )(*parts)
    return out.reshape(matrix.shape)


def solution(mesh):
    in_specs = (P(None, "row", None, None, "col", None), P(None, "row", None, None), P())
    out_specs = P(None, "row", None, None, "col", None)
    return jax.shard_map(
        per_device, mesh=mesh, in_specs=in_specs, out_specs=out_specs, check_vma=False
    )
```

```python
import jax
import jax.numpy as jnp
from jax import lax
from jax.experimental import pallas as pl
from jax.experimental.pallas import tpu as pltpu
from jax.sharding import PartitionSpec as P

F32 = jnp.float32
BF16 = jnp.bfloat16
MESH = pl.DeviceIdType.MESH
NN = (((1,), (0,)), ((), ()))
NT = (((1,), (1,)), ((), ()))
Y, Z, X = 8, 8, 4
VMEM_LIMIT = 24 * 1024 * 1024


def rem(value, by):
    return lax.rem(value, jnp.int32(by))


def div(value, by):
    return lax.div(value, jnp.int32(by))


def split(value):
    high = value.astype(BF16)
    return high, (value - high.astype(F32)).astype(BF16)


def dot3(left, right, dims):
    def dot(a, b):
        return lax.dot_general(a, b, dims, preferred_element_type=F32)

    return dot(left[0], right[0]) + (dot(left[0], right[1]) + dot(left[1], right[0]))


def unit_lower(block):
    i = lax.broadcasted_iota(jnp.int32, block.shape, 0)
    k = lax.broadcasted_iota(jnp.int32, block.shape, 1)
    return jnp.where(i > k, block, jnp.where(i == k, 1.0, 0.0).astype(F32))


def kernel(
    a_hbm, v_hbm, t_hbm, o_s, uh, ul, wh, wl, a_s, v_s, t_s,
    vth, vtl, qt, xbuf, rsrc, rs, cmb, pct, prt, vc, uch, ucl, gsrc, gz, gsum, gx, gt,
    ld_sem, one_s, one_r, v_s_s, v_s_r, v_l, vg_s, vg_r, rs_s, rs_r, y_s, y_r,
    z_s, z_r, gz_s, gz_r, x_s, x_r, f_s, f_r, gx_s, gx_r,
):
    row = lax.axis_index("row")
    col = lax.axis_index("col")
    y, j = div(row, 2), rem(row, 2)
    z, x = div(col, X), rem(col, X)
    half, pos = div(col, 16), rem(col, 16)
    zs = [rem(z + Z - d, Z) for d in range(Z)]
    xs = [rem(x + d, X) for d in range(X)]
    ys = [rem(y + d, Y) for d in range(Y)]

    def flip(index):
        return index + 1 - 2 * rem(index, 2)

    mine = 8 * j + y
    t_target, t_source = (pos, 16 * half + flip(row)), (flip(pos), 16 * half + row)
    partner = (2 * y + 1 - j, col)

    def y_peer(d):
        return (2 * ys[d] + j, col)

    def z_peer(d):
        return (row, X * zs[Z - d] + x)

    def x_peer(d):
        return (row, X * z + xs[d % X])

    owner = row == pos

    def v_piece(d, lane):
        return v_s.at[half + 2 * lane, rows(32 * ys[d], 32)], 256 * lane + 32 * ys[d]

    def v_scatter(d, lane, same):
        src, start = v_piece(d, lane)
        return pltpu.make_async_remote_copy(
            src_ref=src, dst_ref=vc.at[rows(start, 32)],
            send_sem=v_s_s.at[d, same], recv_sem=v_s_r,
            device_id={"row": 2 * ys[d] + lane, "col": col}, device_id_type=MESH,
        )

    def v_local():
        src, start = v_piece(0, j)
        return pltpu.make_async_copy(src, vc.at[rows(start, 32)], v_l)

    def rows(start, size, step=16):
        return pl.ds(pl.multiple_of(start, step), size)

    started = []

    def send(src, dst, ssem, rsem, target):
        copy = pltpu.make_async_remote_copy(
            src_ref=src, dst_ref=dst, send_sem=ssem, recv_sem=rsem,
            device_id={"row": target[0], "col": target[1]}, device_id_type=MESH,
        )
        copy.start()
        started.append(copy)
        return copy

    loads = [
        pltpu.make_async_copy(src, dst, ld_sem.at[i])
        for i, (src, dst) in enumerate([(v_hbm, v_s), (a_hbm, a_s), (t_hbm, t_s)])
    ]
    for copy in loads:
        copy.start()
    barrier = pltpu.get_barrier_semaphore()
    greeted = (
        [y_peer(d) for d in range(1, Y)] + [z_peer(d) for d in range(1, Z)]
        + [x_peer(d) for d in range(1, X)] + [partner, t_source]
        + [(2 * ys[d] + 1 - j, col) for d in range(1, Y)]
    )
    for peer in greeted:
        pl.semaphore_signal(
            barrier, inc=1, device_id={"row": peer[0], "col": peer[1]}, device_id_type=MESH
        )

    loads[0].wait()
    for lr in range(4):
        block = v_s[lr]
        if lr == 0:
            block = jnp.where(row == 0, unit_lower(block), block)
        high, low = split(block.T)
        vth[:, 256 * lr : 256 * lr + 256] = high
        vtl[:, 256 * lr : 256 * lr + 256] = low
        high, low = split(block)
        uh[lr] = high
        ul[lr] = low

    loads[1].wait()

    def partial(lc):
        block = jnp.concatenate(
            [a_s[pl.ds(2 * lc + q, 1024, stride=4), :] for q in range(2)], axis=1
        )
        qt[lc] = dot3((vth[...], vtl[...]), split(block), NN)

    def swap_of(lc):
        return send(
            qt.at[lc, rows(128 * (1 - j), 128)], xbuf.at[lc],
            one_s.at[lc], one_r.at[lc], partner,
        )

    order = (4, 3, 5, 2, 6, 1, 7)

    partial(0)
    pl.semaphore_wait(barrier, len(greeted))
    swaps = [swap_of(0)]

    @pl.when(owner)
    def _():
        v_local().start()
        for d in (4, 3, 5, 2, 6, 1, 7, 0):
            v_scatter(d, 1 - j, 1).start()
            if d:
                v_scatter(d, j, 0).start()

    partial(1)
    swaps.append(swap_of(1))
    def own_part(lc, d):
        return rsrc[lc, rows(16 * ys[d % Y], 16), :]

    def scatter(lc, slot, src, d):
        hops[lc][slot] = send(
            src, rs.at[lc, slot], rs_s.at[lc, slot], rs_r.at[lc, slot], y_peer(d)
        )

    def add_and_pass(lc, arrived, chunk, slot, d):
        hops[lc][arrived].wait_recv()
        part = cmb.at[lc, slot - 4]
        part[...] = own_part(lc, chunk) + rs[lc, arrived]
        scatter(lc, slot, part, d)

    hops = [{}, {}]
    for lc in range(2):
        swaps[lc].wait_recv()
        rsrc[lc] = qt[lc, rows(128 * j, 128), :] + xbuf[lc]
        for slot, chunk, d in ((0, -4, 7), (1, 3, 1), (2, -1, 7), (3, 1, 1)):
            scatter(lc, slot, rsrc.at[lc, rows(16 * ys[chunk % Y], 16)], d)
    loads[2].wait()
    factor = split(t_s[...])
    for lr in range(4):
        high, low = split(dot3((uh[lr], ul[lr]), factor, NT))
        uh[lr] = high
        ul[lr] = low
    own = rows(16 * mine, 16)
    t_z, t_x = 4 * half + div(flip(row), X), rem(flip(row), X)
    for lc in range(2):
        add_and_pass(lc, 0, -3, 4, 7)
        add_and_pass(lc, 1, 2, 5, 2)
    for lc in range(2):
        add_and_pass(lc, 4, -2, 6, 6)
    @pl.when(owner)
    def _():
        v_local().wait()

    @pl.when(jnp.logical_not(owner))
    def _():
        v_scatter(0, j, 0).wait_recv()

    def v_row(d):
        return vc.at[rows(256 * j + 32 * ys[d % Y], 32)]

    def v_send(src, slot, d):
        v_gather[slot] = send(src, src, vg_s.at[slot], vg_r.at[slot], y_peer(d))

    v_gather = {}
    for d in (2, 6, 1, 7):
        v_send(v_row(0), d, d)
    totals, t_moves = [], []
    for lc in range(2):
        total = own_part(lc, 0)
        for slot in (2, 3, 5, 6):
            hops[lc][slot].wait_recv()
            total = total + rs[lc, slot]
        pct[lc, own, :] = total
        totals.append(total)
        t_moves.append(send(
            pct.at[lc, own], prt.at[lc, t_z, t_x], one_s.at[2 + lc], one_r.at[2 + lc], t_target
        ))
    v_gather[2].wait_recv()
    v_send(v_row(-2), 3, 1)
    v_send(v_row(-2), 4, 2)
    v_gather[6].wait_recv()
    v_send(v_row(2), 5, 7)
    def x_send(d, lc):
        part = prt.at[lc, zs[d], x]
        return [
            send(part, part, x_s.at[side, lc, d], x_r.at[side, lc, d], x_peer(1 - 2 * side))
            for side in range(2)
        ]

    near = (2, 6, 1, 7, 3, 5, 4)

    def z_take(d, lc):
        z_gather[lc][d].wait_recv()
        for origin, later, hop in ((2, 3, 1), (2, 4, 2), (6, 5, 7)):
            if d == origin:
                part = prt.at[lc, zs[d], x]
                z_gather[lc][later] = send(
                    part, part, z_s.at[lc, later], z_r.at[lc, later], z_peer(hop)
                )
        x_gather[lc][d] = x_send(d, lc)

    z_gather, x_gather = [], [{}, {}]
    def z_start(lc):
        t_moves[lc].wait_recv()
        chunk = prt.at[lc, z, x]
        z_gather.append({
            d: send(chunk, chunk, z_s.at[lc, d], z_r.at[lc, d], z_peer(d)) for d in (2, 6, 1, 7)
        })
        x_gather[lc][0] = x_send(0, lc)

    z_start(0)
    for d in (1, 7, 3, 5, 4):
        v_gather[d].wait_recv()
    v_half = vc.at[rows(256 * j, 256)]
    v_swap = send(v_half, v_half, one_s.at[4], one_r.at[4], partner)
    z_start(1)
    v_swap.wait_recv()
    first = vc[0:256, :]
    first = jnp.where(col == 0, unit_lower(first), first)
    v_cols = [split(first), split(vc[256:512, :])]
    gsrc[...] = dot3(split(totals[0]), v_cols[0], NN) + dot3(split(totals[1]), v_cols[1], NN)
    g_z = [send(gsrc, gz.at[d], gz_s.at[d], gz_r.at[d], z_peer(d)) for d in order]
    p_part = pct.at[:, own]
    p_gather = [
        send(p_part, p_part, y_s.at[0, d], y_r.at[0, d], y_peer(d)) for d in order
    ]
    for lc in range(2):
        high, low = split(dot3(factor, v_cols[lc], NT))
        uch[:, 256 * lc : 256 * lc + 256] = high
        ucl[:, 256 * lc : 256 * lc + 256] = low

    forward = [[], []]

    def pass_on(d, lc):
        x_gather[lc][d][lc].wait_recv()
        part = prt.at[lc, zs[d], xs[3 - 2 * lc]]
        forward[lc].append(
            send(part, part, f_s.at[lc, d], f_r.at[lc, d], x_peer(1 - 2 * lc))
        )

    for lc in range(2):
        for d in near[:4]:
            z_take(d, lc)
    part_sum = gsrc[...]
    for copy, d in zip(g_z, order):
        copy.wait_recv()
        part_sum = part_sum + gz[d]
    gsum[...] = part_sum
    g_x = [
        send(gsum, gx.at[d], gx_s.at[d], gx_r.at[d], x_peer(d)) for d in range(1, X)
    ]
    for d in (0,) + near[:4]:
        pass_on(d, 0)
    for lc in range(2):
        for d in near[4:]:
            z_take(d, lc)
    for d, copy in zip(range(1, X), g_x):
        copy.wait_recv()
        part_sum = part_sum + gx[d]
    gt[own, :] = part_sum
    g_gather = [
        send(gt.at[own], gt.at[own], y_s.at[1, d], y_r.at[1, d], y_peer(d)) for d in order
    ]
    for d in near[4:]:
        pass_on(d, 0)
    for d in (0,) + near:
        pass_on(d, 1)
    for copy in p_gather:
        copy.wait_recv()
    p_half = pct.at[:, rows(128 * j, 128)]
    p_swap = send(p_half, p_half, one_s.at[5], one_r.at[5], partner)

    for copy in g_gather:
        copy.wait_recv()
    g_half = gt.at[rows(128 * j, 128)]
    g_swap = send(g_half, g_half, one_s.at[6], one_r.at[6], partner)
    places = [(2 * (e % 8) + e // 8) ^ 1 for e in range(16)]
    for lc in range(2):
        for d in (0,) + near:
            x_gather[lc][d][1 - lc].wait_recv()
        for copy in forward[lc]:
            copy.wait_recv()
        for h in range(2):
            lr = h + 2 * lc
            left = split(jnp.concatenate(
                [prt[lc, 4 * h + p // X, p % X] for p in places], axis=0
            ).T)
            for oc in range(2):
                cols = slice(256 * oc, 256 * oc + 256)
                delta = dot3(left, (uch[:, cols], ucl[:, cols]), NN)
                for q in range(2):
                    where = pl.ds(lr * 1024 + 2 * oc + q, 256, stride=4)
                    o_s[where, :] = a_s[where, :] - delta[:, 128 * q : 128 * q + 128]
    p_swap.wait_recv()
    g_swap.wait_recv()
    inner = split(gt[...])
    for lc in range(2):
        cols = slice(256 * lc, 256 * lc + 256)
        high, low = split(pct[lc] - dot3(inner, (uch[:, cols], ucl[:, cols]), NN))
        wh[:, cols] = high
        wl[:, cols] = low
    for copy in started:
        copy.wait_send()

    @pl.when(owner)
    def _():
        for d in range(Y):
            v_scatter(d, 1 - j, 1).wait_send()
            if d:
                v_scatter(d, j, 0).wait_send()


def finish_kernel(o_ref, uh_ref, ul_ref, wh_ref, wl_ref, out_hbm, buf, sems):
    def store(lr):
        part = pl.ds(1024 * lr, 1024)
        return pltpu.make_async_copy(buf.at[part], out_hbm.at[part], sems.at[lr])

    right = [
        (wh_ref[:, 256 * oc : 256 * oc + 256], wl_ref[:, 256 * oc : 256 * oc + 256])
        for oc in range(2)
    ]
    for lr in range(4):
        left = (uh_ref[lr], ul_ref[lr])
        for oc in range(2):
            delta = dot3(left, right[oc], NN)
            for q in range(2):
                where = pl.ds(1024 * lr + 2 * oc + q, 256, stride=4)
                buf[where, :] = o_ref[where, :] - delta[:, 128 * q : 128 * q + 128]
        store(lr).start()
    for lr in range(4):
        store(lr).wait()


def per_device(matrix, vectors, t_factor):
    a = matrix.reshape(4096, 128)
    v = vectors.reshape(4, 256, 256)
    vm = pltpu.VMEM
    dma = pltpu.SemaphoreType.DMA
    shape = jax.ShapeDtypeStruct
    parts = pl.pallas_call(
        kernel,
        out_shape=[
            shape((4096, 128), F32), shape((4, 256, 256), BF16), shape((4, 256, 256), BF16),
            shape((256, 512), BF16), shape((256, 512), BF16),
        ],
        in_specs=[pl.BlockSpec(memory_space=pl.ANY)] * 3,
        out_specs=[pl.BlockSpec(memory_space=pltpu.VMEM)] * 5,
        scratch_shapes=[
            vm((4096, 128), F32), vm((4, 256, 256), F32), vm((256, 256), F32),
            vm((256, 1024), BF16), vm((256, 1024), BF16),
            vm((2, 256, 256), F32), vm((2, 128, 256), F32), vm((2, 128, 256), F32),
            vm((2, 8, 16, 256), F32), vm((2, 3, 16, 256), F32), vm((2, 256, 256), F32), vm((2, 8, 4, 16, 256), F32),
            vm((512, 256), F32), vm((256, 512), BF16), vm((256, 512), BF16),
            vm((16, 256), F32), vm((8, 16, 256), F32), vm((16, 256), F32),
            vm((4, 16, 256), F32), vm((256, 256), F32),
            dma((3,)), dma((7,)), dma((7,)), dma((8, 2)), dma, dma, dma((8,)), dma((8,)),
            dma((2, 8)), dma((2, 8)), dma((2, 8)), dma((2, 8)),
            dma((2, 8)), dma((2, 8)), dma((8,)), dma((8,)),
            dma((2, 2, 8)), dma((2, 2, 8)), dma((2, 8)), dma((2, 8)), dma((4,)), dma((4,)),
        ],
        compiler_params=pltpu.CompilerParams(
            collective_id=0, has_side_effects=True, vmem_limit_bytes=VMEM_LIMIT
        ),
        name="band_update",
    )(*[pltpu.with_memory_space_constraint(arg, pltpu.HBM) for arg in (a, v, t_factor)])
    out = pl.pallas_call(
        finish_kernel,
        out_shape=shape((4096, 128), F32),
        in_specs=[pl.BlockSpec(memory_space=pltpu.VMEM)] * 5,
        out_specs=pl.BlockSpec(memory_space=pl.ANY),
        scratch_shapes=[vm((4096, 128), F32), dma((4,))],
        compiler_params=pltpu.CompilerParams(vmem_limit_bytes=VMEM_LIMIT // 2),
        name="band_finish",
    )(*parts)
    return out.reshape(matrix.shape)


def solution(mesh):
    in_specs = (P(None, "row", None, None, "col", None), P(None, "row", None, None), P())
    out_specs = P(None, "row", None, None, "col", None)
    return jax.shard_map(
        per_device, mesh=mesh, in_specs=in_specs, out_specs=out_specs, check_vma=False
    )
```

```python
import jax
import jax.numpy as jnp
from jax import lax
from jax.experimental import pallas as pl
from jax.experimental.pallas import tpu as pltpu
from jax.sharding import PartitionSpec as P

F32 = jnp.float32
BF16 = jnp.bfloat16
MESH = pl.DeviceIdType.MESH
NN = (((1,), (0,)), ((), ()))
NT = (((1,), (1,)), ((), ()))
Y, Z, X = 8, 8, 4
VMEM_LIMIT = 24 * 1024 * 1024


def rem(value, by):
    return lax.rem(value, jnp.int32(by))


def div(value, by):
    return lax.div(value, jnp.int32(by))


def split(value):
    high = value.astype(BF16)
    return high, (value - high.astype(F32)).astype(BF16)


def dot3(left, right, dims):
    def dot(a, b):
        return lax.dot_general(a, b, dims, preferred_element_type=F32)

    return dot(left[0], right[0]) + (dot(left[0], right[1]) + dot(left[1], right[0]))


def unit_lower(block):
    i = lax.broadcasted_iota(jnp.int32, block.shape, 0)
    k = lax.broadcasted_iota(jnp.int32, block.shape, 1)
    return jnp.where(i > k, block, jnp.where(i == k, 1.0, 0.0).astype(F32))


def kernel(
    a_hbm, v_hbm, t_hbm, o_s, uh, ul, wh, wl, a_s, v_s, t_s,
    vth, vtl, qt, xbuf, rsrc, rs, cmb, pct, prt, vc, uch, ucl, gsrc, gz, gsum, gx, gt,
    ld_sem, one_s, one_r, v_s_s, v_s_r, v_l, vg_s, vg_r, rs_s, rs_r, y_s, y_r,
    z_s, z_r, gz_s, gz_r, x_s, x_r, f_s, f_r, gx_s, gx_r,
):
    row = lax.axis_index("row")
    col = lax.axis_index("col")
    y, j = div(row, 2), rem(row, 2)
    z, x = div(col, X), rem(col, X)
    half, pos = div(col, 16), rem(col, 16)
    zs = [rem(z + Z - d, Z) for d in range(Z)]
    xs = [rem(x + d, X) for d in range(X)]
    ys = [rem(y + d, Y) for d in range(Y)]

    def flip(index):
        return index + 1 - 2 * rem(index, 2)

    mine = 8 * j + y
    t_target, t_source = (pos, 16 * half + flip(row)), (flip(pos), 16 * half + row)
    partner = (2 * y + 1 - j, col)

    def y_peer(d):
        return (2 * ys[d] + j, col)

    def z_peer(d):
        return (row, X * zs[Z - d] + x)

    def x_peer(d):
        return (row, X * z + xs[d % X])

    owner = row == pos

    def v_piece(d, lane):
        return v_s.at[half + 2 * lane, rows(32 * ys[d], 32)], 256 * lane + 32 * ys[d]

    def v_scatter(d, lane, same):
        src, start = v_piece(d, lane)
        return pltpu.make_async_remote_copy(
            src_ref=src, dst_ref=vc.at[rows(start, 32)],
            send_sem=v_s_s.at[d, same], recv_sem=v_s_r,
            device_id={"row": 2 * ys[d] + lane, "col": col}, device_id_type=MESH,
        )

    def v_local():
        src, start = v_piece(0, j)
        return pltpu.make_async_copy(src, vc.at[rows(start, 32)], v_l)

    def rows(start, size, step=16):
        return pl.ds(pl.multiple_of(start, step), size)

    started = []

    def send(src, dst, ssem, rsem, target):
        copy = pltpu.make_async_remote_copy(
            src_ref=src, dst_ref=dst, send_sem=ssem, recv_sem=rsem,
            device_id={"row": target[0], "col": target[1]}, device_id_type=MESH,
        )
        copy.start()
        started.append(copy)
        return copy

    loads = [
        pltpu.make_async_copy(src, dst, ld_sem.at[i])
        for i, (src, dst) in enumerate([(v_hbm, v_s), (a_hbm, a_s), (t_hbm, t_s)])
    ]
    for copy in loads:
        copy.start()
    barrier = pltpu.get_barrier_semaphore()
    greeted = (
        [y_peer(d) for d in range(1, Y)] + [z_peer(d) for d in range(1, Z)]
        + [x_peer(d) for d in range(1, X)] + [partner, t_source]
        + [(2 * ys[d] + 1 - j, col) for d in range(1, Y)]
    )
    for peer in greeted:
        pl.semaphore_signal(
            barrier, inc=1, device_id={"row": peer[0], "col": peer[1]}, device_id_type=MESH
        )

    loads[0].wait()
    for lr in range(4):
        block = v_s[lr]
        if lr == 0:
            block = jnp.where(row == 0, unit_lower(block), block)
        high, low = split(block.T)
        vth[:, 256 * lr : 256 * lr + 256] = high
        vtl[:, 256 * lr : 256 * lr + 256] = low
        high, low = split(block)
        uh[lr] = high
        ul[lr] = low

    loads[1].wait()

    def partial(lc):
        block = jnp.concatenate(
            [a_s[pl.ds(2 * lc + q, 1024, stride=4), :] for q in range(2)], axis=1
        )
        qt[lc] = dot3((vth[...], vtl[...]), split(block), NN)

    def swap_of(lc):
        return send(
            qt.at[lc, rows(128 * (1 - j), 128)], xbuf.at[lc],
            one_s.at[lc], one_r.at[lc], partner,
        )

    order = (4, 3, 5, 2, 6, 1, 7)

    partial(0)
    pl.semaphore_wait(barrier, len(greeted))
    swaps = [swap_of(0)]

    @pl.when(owner)
    def _():
        v_local().start()
        for d in (4, 3, 5, 2, 6, 1, 7, 0):
            v_scatter(d, 1 - j, 1).start()
            if d:
                v_scatter(d, j, 0).start()

    partial(1)
    swaps.append(swap_of(1))
    def own_part(lc, d):
        return rsrc[lc, rows(16 * ys[d % Y], 16), :]

    def scatter(lc, slot, src, d):
        hops[lc][slot] = send(
            src, rs.at[lc, slot], rs_s.at[lc, slot], rs_r.at[lc, slot], y_peer(d)
        )

    def add_and_pass(lc, arrived, chunk, slot, d):
        hops[lc][arrived].wait_recv()
        part = cmb.at[lc, slot - 4]
        part[...] = own_part(lc, chunk) + rs[lc, arrived]
        scatter(lc, slot, part, d)

    hops = [{}, {}]
    for lc in range(2):
        swaps[lc].wait_recv()
        rsrc[lc] = qt[lc, rows(128 * j, 128), :] + xbuf[lc]
        for slot, chunk, d in ((0, -4, 7), (1, 3, 1), (2, -1, 7), (3, 1, 1)):
            scatter(lc, slot, rsrc.at[lc, rows(16 * ys[chunk % Y], 16)], d)
    loads[2].wait()
    factor = split(t_s[...])
    for lr in range(4):
        high, low = split(dot3((uh[lr], ul[lr]), factor, NT))
        uh[lr] = high
        ul[lr] = low
    own = rows(16 * mine, 16)
    t_z, t_x = 4 * half + div(flip(row), X), rem(flip(row), X)
    for lc in range(2):
        add_and_pass(lc, 0, -3, 4, 7)
        add_and_pass(lc, 1, 2, 5, 2)
    for lc in range(2):
        add_and_pass(lc, 4, -2, 6, 6)
    @pl.when(owner)
    def _():
        v_local().wait()

    @pl.when(jnp.logical_not(owner))
    def _():
        v_scatter(0, j, 0).wait_recv()

    def v_row(d):
        return vc.at[rows(256 * j + 32 * ys[d % Y], 32)]

    def v_send(src, slot, d):
        v_gather[slot] = send(src, src, vg_s.at[slot], vg_r.at[slot], y_peer(d))

    v_gather = {}
    for d in (2, 6, 1, 7):
        v_send(v_row(0), d, d)
    totals, t_moves = [], []
    for lc in range(2):
        total = own_part(lc, 0)
        for slot in (2, 3, 5, 6):
            hops[lc][slot].wait_recv()
            total = total + rs[lc, slot]
        pct[lc, own, :] = total
        totals.append(total)
        t_moves.append(send(
            pct.at[lc, own], prt.at[lc, t_z, t_x], one_s.at[2 + lc], one_r.at[2 + lc], t_target
        ))
    v_gather[2].wait_recv()
    v_send(v_row(-2), 3, 1)
    v_send(v_row(-2), 4, 2)
    v_gather[6].wait_recv()
    v_send(v_row(2), 5, 7)
    def x_send(d, lc):
        part = prt.at[lc, zs[d], x]
        return [
            send(part, part, x_s.at[side, lc, d], x_r.at[side, lc, d], x_peer(1 - 2 * side))
            for side in range(2)
        ]

    near = (2, 6, 1, 7, 3, 5, 4)

    def z_take(d, lc):
        z_gather[lc][d].wait_recv()
        for origin, later, hop in ((2, 3, 1), (2, 4, 2), (6, 5, 7)):
            if d == origin:
                part = prt.at[lc, zs[d], x]
                z_gather[lc][later] = send(
                    part, part, z_s.at[lc, later], z_r.at[lc, later], z_peer(hop)
                )
        x_gather[lc][d] = x_send(d, lc)

    z_gather, x_gather = [], [{}, {}]
    def z_start(lc):
        t_moves[lc].wait_recv()
        chunk = prt.at[lc, z, x]
        z_gather.append({
            d: send(chunk, chunk, z_s.at[lc, d], z_r.at[lc, d], z_peer(d)) for d in (2, 6, 1, 7)
        })
        x_gather[lc][0] = x_send(0, lc)

    z_start(0)
    for d in (1, 7, 3, 5, 4):
        v_gather[d].wait_recv()
    v_half = vc.at[rows(256 * j, 256)]
    v_swap = send(v_half, v_half, one_s.at[4], one_r.at[4], partner)
    z_start(1)
    v_swap.wait_recv()
    first = vc[0:256, :]
    first = jnp.where(col == 0, unit_lower(first), first)
    v_cols = [split(first), split(vc[256:512, :])]
    gsrc[...] = dot3(split(totals[0]), v_cols[0], NN) + dot3(split(totals[1]), v_cols[1], NN)
    g_x = [
        send(gsrc, gx.at[d], gx_s.at[d], gx_r.at[d], x_peer(d)) for d in range(1, X)
    ]
    p_part = pct.at[:, own]
    p_gather = [
        send(p_part, p_part, y_s.at[0, d], y_r.at[0, d], y_peer(d)) for d in order
    ]
    for lc in range(2):
        high, low = split(dot3(factor, v_cols[lc], NT))
        uch[:, 256 * lc : 256 * lc + 256] = high
        ucl[:, 256 * lc : 256 * lc + 256] = low

    forward = [[], []]

    def pass_on(d, lc):
        x_gather[lc][d][lc].wait_recv()
        part = prt.at[lc, zs[d], xs[3 - 2 * lc]]
        forward[lc].append(
            send(part, part, f_s.at[lc, d], f_r.at[lc, d], x_peer(1 - 2 * lc))
        )

    for d in near[:4]:
        z_take(d, 0)
    part_sum = gsrc[...]
    for d, copy in zip(range(1, X), g_x):
        copy.wait_recv()
        part_sum = part_sum + gx[d]
    gsum[...] = part_sum
    g_z = [send(gsum, gz.at[d], gz_s.at[d], gz_r.at[d], z_peer(d)) for d in order]
    for d in near[:4]:
        z_take(d, 1)
    for d in (0,) + near[:4]:
        pass_on(d, 0)
    for lc in range(2):
        for d in near[4:]:
            z_take(d, lc)
    for copy, d in zip(g_z, order):
        copy.wait_recv()
        part_sum = part_sum + gz[d]
    gt[own, :] = part_sum
    g_gather = [
        send(gt.at[own], gt.at[own], y_s.at[1, d], y_r.at[1, d], y_peer(d)) for d in order
    ]
    for d in near[4:]:
        pass_on(d, 0)
    for d in (0,) + near:
        pass_on(d, 1)
    for copy in p_gather:
        copy.wait_recv()
    p_half = pct.at[:, rows(128 * j, 128)]
    p_swap = send(p_half, p_half, one_s.at[5], one_r.at[5], partner)

    for copy in g_gather:
        copy.wait_recv()
    g_half = gt.at[rows(128 * j, 128)]
    g_swap = send(g_half, g_half, one_s.at[6], one_r.at[6], partner)
    places = [(2 * (e % 8) + e // 8) ^ 1 for e in range(16)]
    for lc in range(2):
        for d in (0,) + near:
            x_gather[lc][d][1 - lc].wait_recv()
        for copy in forward[lc]:
            copy.wait_recv()
        for h in range(2):
            lr = h + 2 * lc
            left = split(jnp.concatenate(
                [prt[lc, 4 * h + p // X, p % X] for p in places], axis=0
            ).T)
            for oc in range(2):
                cols = slice(256 * oc, 256 * oc + 256)
                delta = dot3(left, (uch[:, cols], ucl[:, cols]), NN)
                for q in range(2):
                    where = pl.ds(lr * 1024 + 2 * oc + q, 256, stride=4)
                    o_s[where, :] = a_s[where, :] - delta[:, 128 * q : 128 * q + 128]
    p_swap.wait_recv()
    g_swap.wait_recv()
    inner = split(gt[...])
    for lc in range(2):
        cols = slice(256 * lc, 256 * lc + 256)
        high, low = split(pct[lc] - dot3(inner, (uch[:, cols], ucl[:, cols]), NN))
        wh[:, cols] = high
        wl[:, cols] = low
    for copy in started:
        copy.wait_send()

    @pl.when(owner)
    def _():
        for d in range(Y):
            v_scatter(d, 1 - j, 1).wait_send()
            if d:
                v_scatter(d, j, 0).wait_send()


def finish_kernel(o_ref, uh_ref, ul_ref, wh_ref, wl_ref, out_hbm, buf, sems):
    def store(lr):
        part = pl.ds(1024 * lr, 1024)
        return pltpu.make_async_copy(buf.at[part], out_hbm.at[part], sems.at[lr])

    right = [
        (wh_ref[:, 256 * oc : 256 * oc + 256], wl_ref[:, 256 * oc : 256 * oc + 256])
        for oc in range(2)
    ]
    for lr in range(4):
        left = (uh_ref[lr], ul_ref[lr])
        for oc in range(2):
            delta = dot3(left, right[oc], NN)
            for q in range(2):
                where = pl.ds(1024 * lr + 2 * oc + q, 256, stride=4)
                buf[where, :] = o_ref[where, :] - delta[:, 128 * q : 128 * q + 128]
        store(lr).start()
    for lr in range(4):
        store(lr).wait()


def per_device(matrix, vectors, t_factor):
    a = matrix.reshape(4096, 128)
    v = vectors.reshape(4, 256, 256)
    vm = pltpu.VMEM
    dma = pltpu.SemaphoreType.DMA
    shape = jax.ShapeDtypeStruct
    parts = pl.pallas_call(
        kernel,
        out_shape=[
            shape((4096, 128), F32), shape((4, 256, 256), BF16), shape((4, 256, 256), BF16),
            shape((256, 512), BF16), shape((256, 512), BF16),
        ],
        in_specs=[pl.BlockSpec(memory_space=pl.ANY)] * 3,
        out_specs=[pl.BlockSpec(memory_space=pltpu.VMEM)] * 5,
        scratch_shapes=[
            vm((4096, 128), F32), vm((4, 256, 256), F32), vm((256, 256), F32),
            vm((256, 1024), BF16), vm((256, 1024), BF16),
            vm((2, 256, 256), F32), vm((2, 128, 256), F32), vm((2, 128, 256), F32),
            vm((2, 8, 16, 256), F32), vm((2, 3, 16, 256), F32), vm((2, 256, 256), F32), vm((2, 8, 4, 16, 256), F32),
            vm((512, 256), F32), vm((256, 512), BF16), vm((256, 512), BF16),
            vm((16, 256), F32), vm((8, 16, 256), F32), vm((16, 256), F32),
            vm((4, 16, 256), F32), vm((256, 256), F32),
            dma((3,)), dma((7,)), dma((7,)), dma((8, 2)), dma, dma, dma((8,)), dma((8,)),
            dma((2, 8)), dma((2, 8)), dma((2, 8)), dma((2, 8)),
            dma((2, 8)), dma((2, 8)), dma((8,)), dma((8,)),
            dma((2, 2, 8)), dma((2, 2, 8)), dma((2, 8)), dma((2, 8)), dma((4,)), dma((4,)),
        ],
        compiler_params=pltpu.CompilerParams(
            collective_id=0, has_side_effects=True, vmem_limit_bytes=VMEM_LIMIT
        ),
        name="band_update",
    )(*[pltpu.with_memory_space_constraint(arg, pltpu.HBM) for arg in (a, v, t_factor)])
    out = pl.pallas_call(
        finish_kernel,
        out_shape=shape((4096, 128), F32),
        in_specs=[pl.BlockSpec(memory_space=pltpu.VMEM)] * 5,
        out_specs=pl.BlockSpec(memory_space=pl.ANY),
        scratch_shapes=[vm((4096, 128), F32), dma((4,))],
        compiler_params=pltpu.CompilerParams(vmem_limit_bytes=VMEM_LIMIT // 2),
        name="band_finish",
    )(*parts)
    return out.reshape(matrix.shape)


def solution(mesh):
    in_specs = (P(None, "row", None, None, "col", None), P(None, "row", None, None), P())
    out_specs = P(None, "row", None, None, "col", None)
    return jax.shard_map(
        per_device, mesh=mesh, in_specs=in_specs, out_specs=out_specs, check_vma=False
    )
```

```python
import jax
import jax.numpy as jnp
from jax import lax
from jax.experimental import pallas as pl
from jax.experimental.pallas import tpu as pltpu
from jax.sharding import PartitionSpec as P

F32 = jnp.float32
BF16 = jnp.bfloat16
MESH = pl.DeviceIdType.MESH
NN = (((1,), (0,)), ((), ()))
NT = (((1,), (1,)), ((), ()))
Y, Z, X = 8, 8, 4
VMEM_LIMIT = 24 * 1024 * 1024


def rem(value, by):
    return lax.rem(value, jnp.int32(by))


def div(value, by):
    return lax.div(value, jnp.int32(by))


def split(value):
    high = value.astype(BF16)
    return high, (value - high.astype(F32)).astype(BF16)


def dot3(left, right, dims):
    def dot(a, b):
        return lax.dot_general(a, b, dims, preferred_element_type=F32)

    return dot(left[0], right[0]) + (dot(left[0], right[1]) + dot(left[1], right[0]))


def unit_lower(block):
    i = lax.broadcasted_iota(jnp.int32, block.shape, 0)
    k = lax.broadcasted_iota(jnp.int32, block.shape, 1)
    return jnp.where(i > k, block, jnp.where(i == k, 1.0, 0.0).astype(F32))


def kernel(
    a_hbm, v_hbm, t_hbm, o_s, uh, ul, wh, wl, a_s, v_s, t_s,
    vth, vtl, qt, xbuf, rsrc, rs, cmb, pct, prt, vc, uch, ucl, gsrc, gz, gsum, gx, gt,
    ld_sem, one_s, one_r, v_s_s, v_s_r, v_l, vg_s, vg_r, rs_s, rs_r, y_s, y_r,
    z_s, z_r, gz_s, gz_r, x_s, x_r, f_s, f_r, gx_s, gx_r,
):
    row = lax.axis_index("row")
    col = lax.axis_index("col")
    y, j = div(row, 2), rem(row, 2)
    z, x = div(col, X), rem(col, X)
    half, pos = div(col, 16), rem(col, 16)
    zs = [rem(z + Z - d, Z) for d in range(Z)]
    xs = [rem(x + d, X) for d in range(X)]
    ys = [rem(y + d, Y) for d in range(Y)]

    def flip(index):
        return index + 1 - 2 * rem(index, 2)

    mine = 8 * j + y
    t_target, t_source = (pos, 16 * half + flip(row)), (flip(pos), 16 * half + row)
    partner = (2 * y + 1 - j, col)

    def y_peer(d):
        return (2 * ys[d] + j, col)

    def z_peer(d):
        return (row, X * zs[Z - d] + x)

    def x_peer(d):
        return (row, X * z + xs[d % X])

    owner = row == pos

    def v_piece(d, lane):
        return v_s.at[half + 2 * lane, rows(32 * ys[d], 32)], 256 * lane + 32 * ys[d]

    def v_scatter(d, lane, same):
        src, start = v_piece(d, lane)
        return pltpu.make_async_remote_copy(
            src_ref=src, dst_ref=vc.at[rows(start, 32)],
            send_sem=v_s_s.at[d, same], recv_sem=v_s_r,
            device_id={"row": 2 * ys[d] + lane, "col": col}, device_id_type=MESH,
        )

    def v_local():
        src, start = v_piece(0, j)
        return pltpu.make_async_copy(src, vc.at[rows(start, 32)], v_l)

    def rows(start, size, step=16):
        return pl.ds(pl.multiple_of(start, step), size)

    started = []

    def send(src, dst, ssem, rsem, target):
        copy = pltpu.make_async_remote_copy(
            src_ref=src, dst_ref=dst, send_sem=ssem, recv_sem=rsem,
            device_id={"row": target[0], "col": target[1]}, device_id_type=MESH,
        )
        copy.start()
        started.append(copy)
        return copy

    loads = [
        pltpu.make_async_copy(src, dst, ld_sem.at[i])
        for i, (src, dst) in enumerate([(v_hbm, v_s), (a_hbm, a_s), (t_hbm, t_s)])
    ]
    for copy in loads:
        copy.start()
    barrier = pltpu.get_barrier_semaphore()
    greeted = (
        [y_peer(d) for d in range(1, Y)] + [z_peer(d) for d in range(1, Z)]
        + [x_peer(d) for d in range(1, X)] + [partner, t_source]
        + [(2 * ys[d] + 1 - j, col) for d in range(1, Y)]
    )
    for peer in greeted:
        pl.semaphore_signal(
            barrier, inc=1, device_id={"row": peer[0], "col": peer[1]}, device_id_type=MESH
        )

    loads[0].wait()
    pl.semaphore_wait(barrier, len(greeted))

    @pl.when(owner)
    def _():
        v_local().start()
        for d in (4, 3, 5, 2, 6, 1, 7, 0):
            v_scatter(d, 1 - j, 1).start()
            if d:
                v_scatter(d, j, 0).start()

    for lr in range(4):
        block = v_s[lr]
        if lr == 0:
            block = jnp.where(row == 0, unit_lower(block), block)
        high, low = split(block.T)
        vth[:, 256 * lr : 256 * lr + 256] = high
        vtl[:, 256 * lr : 256 * lr + 256] = low
        high, low = split(block)
        uh[lr] = high
        ul[lr] = low

    loads[1].wait()

    def partial(lc):
        block = jnp.concatenate(
            [a_s[pl.ds(2 * lc + q, 1024, stride=4), :] for q in range(2)], axis=1
        )
        qt[lc] = dot3((vth[...], vtl[...]), split(block), NN)

    def swap_of(lc):
        return send(
            qt.at[lc, rows(128 * (1 - j), 128)], xbuf.at[lc],
            one_s.at[lc], one_r.at[lc], partner,
        )

    order = (4, 3, 5, 2, 6, 1, 7)

    partial(0)
    swaps = [swap_of(0)]

    partial(1)
    swaps.append(swap_of(1))
    def own_part(lc, d):
        return rsrc[lc, rows(16 * ys[d % Y], 16), :]

    def scatter(lc, slot, src, d):
        hops[lc][slot] = send(
            src, rs.at[lc, slot], rs_s.at[lc, slot], rs_r.at[lc, slot], y_peer(d)
        )

    def add_and_pass(lc, arrived, chunk, slot, d):
        hops[lc][arrived].wait_recv()
        part = cmb.at[lc, slot - 4]
        part[...] = own_part(lc, chunk) + rs[lc, arrived]
        scatter(lc, slot, part, d)

    hops = [{}, {}]
    for lc in range(2):
        swaps[lc].wait_recv()
        rsrc[lc] = qt[lc, rows(128 * j, 128), :] + xbuf[lc]
        for slot, chunk, d in ((0, -4, 7), (1, 3, 1), (2, -1, 7), (3, 1, 1)):
            scatter(lc, slot, rsrc.at[lc, rows(16 * ys[chunk % Y], 16)], d)
    loads[2].wait()
    factor = split(t_s[...])
    for lr in range(4):
        high, low = split(dot3((uh[lr], ul[lr]), factor, NT))
        uh[lr] = high
        ul[lr] = low
    own = rows(16 * mine, 16)
    t_z, t_x = 4 * half + div(flip(row), X), rem(flip(row), X)
    for lc in range(2):
        add_and_pass(lc, 0, -3, 4, 7)
        add_and_pass(lc, 1, 2, 5, 2)
    for lc in range(2):
        add_and_pass(lc, 4, -2, 6, 6)
    @pl.when(owner)
    def _():
        v_local().wait()

    @pl.when(jnp.logical_not(owner))
    def _():
        v_scatter(0, j, 0).wait_recv()

    def v_row(d):
        return vc.at[rows(256 * j + 32 * ys[d % Y], 32)]

    def v_send(src, slot, d):
        v_gather[slot] = send(src, src, vg_s.at[slot], vg_r.at[slot], y_peer(d))

    v_gather = {}
    for d in (2, 6, 1, 7):
        v_send(v_row(0), d, d)
    totals, t_moves = [], []
    for lc in range(2):
        total = own_part(lc, 0)
        for slot in (2, 3, 5, 6):
            hops[lc][slot].wait_recv()
            total = total + rs[lc, slot]
        pct[lc, own, :] = total
        totals.append(total)
        t_moves.append(send(
            pct.at[lc, own], prt.at[lc, t_z, t_x], one_s.at[2 + lc], one_r.at[2 + lc], t_target
        ))
    v_gather[2].wait_recv()
    v_send(v_row(-2), 3, 1)
    v_send(v_row(-2), 4, 2)
    v_gather[6].wait_recv()
    v_send(v_row(2), 5, 7)
    def x_send(d, lc):
        part = prt.at[lc, zs[d], x]
        return [
            send(part, part, x_s.at[side, lc, d], x_r.at[side, lc, d], x_peer(1 - 2 * side))
            for side in range(2)
        ]

    near = (2, 6, 1, 7, 3, 5, 4)

    def z_take(d, lc):
        z_gather[lc][d].wait_recv()
        for origin, later, hop in ((2, 3, 1), (2, 4, 2), (6, 5, 7)):
            if d == origin:
                part = prt.at[lc, zs[d], x]
                z_gather[lc][later] = send(
                    part, part, z_s.at[lc, later], z_r.at[lc, later], z_peer(hop)
                )
        x_gather[lc][d] = x_send(d, lc)

    z_gather, x_gather = [], [{}, {}]
    def z_start(lc):
        t_moves[lc].wait_recv()
        chunk = prt.at[lc, z, x]
        z_gather.append({
            d: send(chunk, chunk, z_s.at[lc, d], z_r.at[lc, d], z_peer(d)) for d in (2, 6, 1, 7)
        })
        x_gather[lc][0] = x_send(0, lc)

    z_start(0)
    for d in (1, 7, 3, 5, 4):
        v_gather[d].wait_recv()
    v_half = vc.at[rows(256 * j, 256)]
    v_swap = send(v_half, v_half, one_s.at[4], one_r.at[4], partner)
    z_start(1)
    v_swap.wait_recv()
    first = vc[0:256, :]
    first = jnp.where(col == 0, unit_lower(first), first)
    v_cols = [split(first), split(vc[256:512, :])]
    gsrc[...] = dot3(split(totals[0]), v_cols[0], NN) + dot3(split(totals[1]), v_cols[1], NN)
    g_z = [send(gsrc, gz.at[d], gz_s.at[d], gz_r.at[d], z_peer(d)) for d in order]
    p_part = pct.at[:, own]
    p_gather = [
        send(p_part, p_part, y_s.at[0, d], y_r.at[0, d], y_peer(d)) for d in order
    ]
    forward = [[], []]

    def pass_on(d, lc):
        x_gather[lc][d][lc].wait_recv()
        part = prt.at[lc, zs[d], xs[3 - 2 * lc]]
        forward[lc].append(
            send(part, part, f_s.at[lc, d], f_r.at[lc, d], x_peer(1 - 2 * lc))
        )

    for lc in range(2):
        for d in near[:4]:
            z_take(d, lc)
    part_sum = gsrc[...]
    for copy, d in zip(g_z, order):
        copy.wait_recv()
        part_sum = part_sum + gz[d]
    gsum[...] = part_sum
    g_x = [
        send(gsum, gx.at[d], gx_s.at[d], gx_r.at[d], x_peer(d)) for d in range(1, X)
    ]
    for lc in range(2):
        high, low = split(dot3(factor, v_cols[lc], NT))
        uch[:, 256 * lc : 256 * lc + 256] = high
        ucl[:, 256 * lc : 256 * lc + 256] = low
    for d in (0,) + near[:4]:
        pass_on(d, 0)
    for lc in range(2):
        for d in near[4:]:
            z_take(d, lc)
    for d, copy in zip(range(1, X), g_x):
        copy.wait_recv()
        part_sum = part_sum + gx[d]
    gt[own, :] = part_sum
    g_gather = [
        send(gt.at[own], gt.at[own], y_s.at[1, d], y_r.at[1, d], y_peer(d)) for d in order
    ]
    for d in near[4:]:
        pass_on(d, 0)
    for d in (0,) + near:
        pass_on(d, 1)
    for copy in p_gather:
        copy.wait_recv()
    p_half = pct.at[:, rows(128 * j, 128)]
    p_swap = send(p_half, p_half, one_s.at[5], one_r.at[5], partner)

    for copy in g_gather:
        copy.wait_recv()
    g_half = gt.at[rows(128 * j, 128)]
    g_swap = send(g_half, g_half, one_s.at[6], one_r.at[6], partner)
    places = [(2 * (e % 8) + e // 8) ^ 1 for e in range(16)]
    for lc in range(2):
        for d in (0,) + near:
            x_gather[lc][d][1 - lc].wait_recv()
        for copy in forward[lc]:
            copy.wait_recv()
        for h in range(2):
            lr = h + 2 * lc
            left = split(jnp.concatenate(
                [prt[lc, 4 * h + p // X, p % X] for p in places], axis=0
            ).T)
            for oc in range(2):
                cols = slice(256 * oc, 256 * oc + 256)
                delta = dot3(left, (uch[:, cols], ucl[:, cols]), NN)
                for q in range(2):
                    where = pl.ds(lr * 1024 + 2 * oc + q, 256, stride=4)
                    o_s[where, :] = a_s[where, :] - delta[:, 128 * q : 128 * q + 128]
    p_swap.wait_recv()
    g_swap.wait_recv()
    inner = split(gt[...])
    for lc in range(2):
        cols = slice(256 * lc, 256 * lc + 256)
        high, low = split(pct[lc] - dot3(inner, (uch[:, cols], ucl[:, cols]), NN))
        wh[:, cols] = high
        wl[:, cols] = low
    for copy in started:
        copy.wait_send()

    @pl.when(owner)
    def _():
        for d in range(Y):
            v_scatter(d, 1 - j, 1).wait_send()
            if d:
                v_scatter(d, j, 0).wait_send()


def finish_kernel(o_ref, uh_ref, ul_ref, wh_ref, wl_ref, out_hbm, buf, sems):
    def store(lr):
        part = pl.ds(1024 * lr, 1024)
        return pltpu.make_async_copy(buf.at[part], out_hbm.at[part], sems.at[lr])

    right = [
        (wh_ref[:, 256 * oc : 256 * oc + 256], wl_ref[:, 256 * oc : 256 * oc + 256])
        for oc in range(2)
    ]
    for lr in range(4):
        left = (uh_ref[lr], ul_ref[lr])
        for oc in range(2):
            delta = dot3(left, right[oc], NN)
            for q in range(2):
                where = pl.ds(1024 * lr + 2 * oc + q, 256, stride=4)
                buf[where, :] = o_ref[where, :] - delta[:, 128 * q : 128 * q + 128]
        store(lr).start()
    for lr in range(4):
        store(lr).wait()


def per_device(matrix, vectors, t_factor):
    a = matrix.reshape(4096, 128)
    v = vectors.reshape(4, 256, 256)
    vm = pltpu.VMEM
    dma = pltpu.SemaphoreType.DMA
    shape = jax.ShapeDtypeStruct
    parts = pl.pallas_call(
        kernel,
        out_shape=[
            shape((4096, 128), F32), shape((4, 256, 256), BF16), shape((4, 256, 256), BF16),
            shape((256, 512), BF16), shape((256, 512), BF16),
        ],
        in_specs=[pl.BlockSpec(memory_space=pl.ANY)] * 3,
        out_specs=[pl.BlockSpec(memory_space=pltpu.VMEM)] * 5,
        scratch_shapes=[
            vm((4096, 128), F32), vm((4, 256, 256), F32), vm((256, 256), F32),
            vm((256, 1024), BF16), vm((256, 1024), BF16),
            vm((2, 256, 256), F32), vm((2, 128, 256), F32), vm((2, 128, 256), F32),
            vm((2, 8, 16, 256), F32), vm((2, 3, 16, 256), F32), vm((2, 256, 256), F32), vm((2, 8, 4, 16, 256), F32),
            vm((512, 256), F32), vm((256, 512), BF16), vm((256, 512), BF16),
            vm((16, 256), F32), vm((8, 16, 256), F32), vm((16, 256), F32),
            vm((4, 16, 256), F32), vm((256, 256), F32),
            dma((3,)), dma((7,)), dma((7,)), dma((8, 2)), dma, dma, dma((8,)), dma((8,)),
            dma((2, 8)), dma((2, 8)), dma((2, 8)), dma((2, 8)),
            dma((2, 8)), dma((2, 8)), dma((8,)), dma((8,)),
            dma((2, 2, 8)), dma((2, 2, 8)), dma((2, 8)), dma((2, 8)), dma((4,)), dma((4,)),
        ],
        compiler_params=pltpu.CompilerParams(
            collective_id=0, has_side_effects=True, vmem_limit_bytes=VMEM_LIMIT
        ),
        name="band_update",
    )(*[pltpu.with_memory_space_constraint(arg, pltpu.HBM) for arg in (a, v, t_factor)])
    out = pl.pallas_call(
        finish_kernel,
        out_shape=shape((4096, 128), F32),
        in_specs=[pl.BlockSpec(memory_space=pltpu.VMEM)] * 5,
        out_specs=pl.BlockSpec(memory_space=pl.ANY),
        scratch_shapes=[vm((4096, 128), F32), dma((4,))],
        compiler_params=pltpu.CompilerParams(vmem_limit_bytes=VMEM_LIMIT // 2),
        name="band_finish",
    )(*parts)
    return out.reshape(matrix.shape)


def solution(mesh):
    in_specs = (P(None, "row", None, None, "col", None), P(None, "row", None, None), P())
    out_specs = P(None, "row", None, None, "col", None)
    return jax.shard_map(
        per_device, mesh=mesh, in_specs=in_specs, out_specs=out_specs, check_vma=False
    )
```
